512 devices in a mesh: cells: 128 (over z, y, core), slab: 4 (over x).
Axes of the slice: x: 4, y: 8, z: 8, core: 2. Of those that a mesh axis runs over, the one named last changes fastest.
Arguments:
- centres: float32 [4, 512, 3, 1024], P('slab', 'cells'), may hold values from -6 to 6
- tangents: float32 [4, 512, 3, 1024], P('slab', 'cells'), may hold values from -3.5 to 3.5
- weights: float32 [4, 512, 1024], P('slab', 'cells'), may hold values from -2 to 2
- segment_count: int32 [4, 512], P('slab', 'cells'), may hold values from 512 to 1024
- pairs: int32 [4, 1280, 2], P('slab', 'cells'), may hold values from 0 to 1023, as said below
- pair_count: int32 [4, 128], P('slab', 'cells'), may hold values from 3 to 10, as said below
Outputs:
- grad_centres: float32 [4, 512, 3, 1024], P('slab', 'cells')
- grad_tangents: float32 [4, 512, 3, 1024], P('slab', 'cells')
The draws below stay inside these ranges and needn't reach their ends.
Inputs may be any that keep to these rules, and one draw needn't show every extreme that they name: Slot entries (i, j) of device (s, c): i is a block owned by that device (c * 4 to c * 4 + 3); the block that j names lies within 2 blocks of i in the slab's order; j names the slab above only below the top slab. No unordered block pair is held by two live slots over all devices. Slots at or beyond pair_count also hold pairs that obey these rules. `pair_count`: some device has all 10 slots live.
All inputs are finite; a program needn't handle non-finite values.
Results may differ from the reference program's by a relative error of at most 0.0003.
Values sent between devices are 32-bit elements; how exact they have to be, the bound alone decides.
A program may use at most 64 MiB of HBM per device.

```python
import jax
import jax.numpy as jnp
from jax import lax

BLK = 1024
BLK_DEV = 4
REACH = 2
PMAX = 10
SLABS = 4
SLAB_BLOCKS = 512
N_CELLS = 128


def pair_tables(key):
    cells = SLAB_BLOCKS // BLK_DEV
    extent = 2 * REACH + 1
    candidates = BLK_DEV * extent * 2
    index = jnp.arange(candidates, dtype=jnp.int32)
    local = index // (extent * 2)
    offset = index // 2 % extent - REACH
    upward = index % 2
    slab_index = jnp.arange(SLABS, dtype=jnp.int32)[:, None, None]
    cell_index = jnp.arange(cells, dtype=jnp.int32)[None, :, None]
    first = cell_index * BLK_DEV + local[None, None, :] + 0 * slab_index
    second = first + offset[None, None, :]
    inside = (second >= 0) & (second < SLAB_BLOCKS)
    lower = jnp.minimum(first, second)
    higher = jnp.maximum(first, second)
    parity = (first + second) % 2
    runner = jnp.where(parity == 0, lower // BLK_DEV, higher // BLK_DEV)
    same_ok = inside & (upward[None, None, :] == 0) & (runner == cell_index) & ((offset[None, None, :] >= 0) | (second // BLK_DEV != cell_index))
    cross_ok = inside & (upward[None, None, :] == 1) & (slab_index < SLABS - 1)
    valid = same_ok | cross_ok
    forced = jnp.where((local == 0) & (offset == -1) & (upward == 0), 3, jnp.where((local == BLK_DEV - 1) & (offset == 2) & (upward == 0), 2, jnp.where((local == 0) & (offset == 0) & (upward == 1), 1, 0)))
    forced = jnp.broadcast_to(forced[None, None, :], valid.shape)
    score_key, count_key, busy_key = jax.random.split(key, 3)
    scores = jax.random.randint(score_key, valid.shape, 0, 2 ** 20) * candidates + index[None, None, :]
    big = 2 ** 20 * candidates
    priority = jnp.where(valid & (forced > 0), (2 + forced) * big + index[None, None, :], jnp.where(valid, big + scores, scores))
    chosen = lax.top_k(priority, PMAX)[1]
    picked_first = jnp.take_along_axis(first, chosen, axis=2)
    picked_second = jnp.take_along_axis(second + SLAB_BLOCKS * jnp.broadcast_to(upward[None, None, :], second.shape), chosen, axis=2)
    table = jnp.stack([picked_first, picked_second], axis=-1).reshape(SLABS, cells * PMAX, 2).astype(jnp.int32)
    keys = jax.random.split(count_key, 3)
    draws = [jax.random.randint(one_key, (SLABS * cells,), 0, PMAX - 2) for one_key in keys]
    counts = 3 + jnp.minimum(jnp.minimum(draws[0], draws[1]), draws[2])
    busiest = jax.random.randint(busy_key, (), 0, SLABS * cells)
    counts = counts.at[busiest].set(PMAX)
    return (table, counts.reshape(SLABS, cells).astype(jnp.int32))


def draw_pairs(key, part):
    table, counts = pair_tables(jax.random.fold_in(key, 7))
    return table


def draw_pair_count(key, part):
    table, counts = pair_tables(jax.random.fold_in(key, 7))
    return counts


def with_ends(values, own_key, smallest, top_value):
    place = [jax.random.randint(jax.random.fold_in(own_key, axis), (), 0, length) for axis, length in enumerate(values.shape)]
    widest = values.shape.index(max(values.shape))
    next_to = place[:widest] + [(place[widest] + 1) % values.shape[widest]] + place[widest + 1:]
    return values.at[tuple(place)].set(smallest).at[tuple(next_to)].set(top_value)


def shard_levels(rng, shape, shards, smallest, high):
    def one(axis_at, parts):
        heights = jax.random.uniform(jax.random.fold_in(jax.random.fold_in(rng, 6), axis_at), (parts,), jnp.float32, smallest / len(shards), high / len(shards))
        return jnp.repeat(jnp.exp(heights), shape[axis_at] // parts).reshape((-1,) + (1,) * (len(shape) - axis_at - 1))

    loudness = one(*shards[0])
    for cut in shards[1:]:
        loudness = loudness * one(*cut)
    return loudness


def scatter_about(key, dims, width, limit, cuts=(), kind=jnp.bfloat16):
    level = shard_levels(key, dims, cuts, -0.22, 0.18) if cuts else 1.0
    result = jax.random.normal(key, dims, jnp.float32) * width * level
    return jnp.minimum(jnp.maximum(result, -limit), limit).astype(kind)


def setup_inputs(seed: int = 0) -> dict:
    key_of = jax.random.split(jax.random.key(seed), 7)
    centres = scatter_about(key_of[0], (SLABS, SLAB_BLOCKS, 3, BLK), 1.0, 6.0, ((0, 4), (1, 128)), jnp.float32)
    tangents = scatter_about(key_of[1], (SLABS, SLAB_BLOCKS, 3, BLK), 0.577, 3.5, ((0, 4), (1, 128)), jnp.float32)
    weights = jnp.clip(jax.random.uniform(key_of[2], (SLABS, SLAB_BLOCKS, BLK), jnp.float32, -2.0, 2.0) * shard_levels(key_of[2], (SLABS, SLAB_BLOCKS, BLK), ((0, 4), (1, 128)), -0.4, 0.0), -2.0, 2.0)
    segment_count = with_ends(jax.random.randint(key_of[3], (SLABS, SLAB_BLOCKS), BLK // 2, BLK + 1), jax.random.fold_in(key_of[3], 1), BLK // 2, BLK).astype(jnp.int32)
    pairs = draw_pairs(jax.random.fold_in(key_of[6], 71), 0)
    pair_count = draw_pair_count(jax.random.fold_in(key_of[6], 71), 0)
    return dict(centres=centres, tangents=tangents, weights=weights, segment_count=segment_count, pairs=pairs, pair_count=pair_count)


width_square = 4.0


def tile_terms(left_block, right_block, factor):
    highest = lax.Precision.HIGHEST
    segments = left_block.shape[1]
    row_block = min(512, segments)
    right_pos = right_block[0:3]
    right_dir = right_block[3:6]
    right_weight = right_block[6]
    right_grad = jnp.zeros((6, segments), jnp.float32)
    left_parts = []
    for row_start in range(0, segments, row_block):
        row_part = left_block[:, row_start:row_start + row_block]
        left_pos = row_part[0:3]
        left_dir = row_part[3:6]
        left_weight = row_part[6]
        distance = jnp.sum((left_pos[:, :, None] - right_pos[:, None, :]) ** 2, axis=0)
        gauss = jnp.exp(-distance / width_square)
        cosine = (left_dir[0][:, None] * right_dir[0][None, :]
                  + left_dir[1][:, None] * right_dir[1][None, :]
                  + left_dir[2][:, None] * right_dir[2][None, :])
        first_order = left_weight[:, None] * right_weight[None, :] * gauss * cosine
        second_order = first_order * cosine
        pull = -2.0 * factor / width_square
        left_pos_grad = pull * (left_pos * jnp.sum(second_order, axis=1)[None, :]
                                - jnp.einsum('kb,ab->ka', right_pos, second_order, precision=highest))
        right_pos_grad = pull * (right_pos * jnp.sum(second_order, axis=0)[None, :]
                                 - jnp.einsum('ka,ab->kb', left_pos, second_order, precision=highest))
        left_dir_grad = 2.0 * factor * jnp.einsum('kb,ab->ka', right_dir, first_order, precision=highest)
        right_dir_grad = 2.0 * factor * jnp.einsum('ka,ab->kb', left_dir, first_order, precision=highest)
        left_parts.append(jnp.concatenate([left_pos_grad, left_dir_grad], axis=0))
        right_grad = right_grad + jnp.concatenate([right_pos_grad, right_dir_grad], axis=0)
    return jnp.concatenate(left_parts, axis=1), right_grad


def reference(centres, tangents, weights, segment_count, pairs, pair_count):
    loss_scale = BLK ** -0.5
    blocks_all = SLABS * SLAB_BLOCKS
    live_segment = jnp.arange(BLK)[None, None, :] < segment_count[:, :, None]
    masked = jnp.where(live_segment, weights, jnp.zeros_like(weights))
    stacked = jnp.concatenate([centres, tangents, masked[:, :, None, :]], axis=2).reshape(blocks_all, 7, BLK)
    offsets = (jnp.arange(SLABS) * SLAB_BLOCKS).astype(jnp.int32)[:, None]
    first = (pairs[:, :, 0] + offsets).reshape(-1).astype(jnp.int32)
    second = (pairs[:, :, 1] + offsets).reshape(-1).astype(jnp.int32)
    slot_index = jnp.arange(N_CELLS * PMAX)
    live = (slot_index % PMAX)[None, :] < pair_count[:, slot_index // PMAX]
    factor = (loss_scale * jnp.where(pairs[:, :, 0] == pairs[:, :, 1], 1.0, 2.0)).reshape(-1)
    live_flat = live.reshape(-1)
    order = jnp.argsort(jnp.logical_not(live_flat).astype(jnp.int32), stable=True).astype(jnp.int32)
    live_total = jnp.sum(live_flat.astype(jnp.int32))

    def one_pair(position, totals):
        picked = order[position]
        left_index = first[picked]
        right_index = second[picked]
        left_block = lax.dynamic_index_in_dim(stacked, left_index, 0, keepdims=False)
        right_block = lax.dynamic_index_in_dim(stacked, right_index, 0, keepdims=False)
        left_grad, right_grad = tile_terms(left_block, right_block, factor[picked])
        totals = totals.at[left_index].add(left_grad)
        totals = totals.at[right_index].add(right_grad)
        return totals

    totals = lax.fori_loop(0, live_total, one_pair, jnp.zeros((blocks_all, 6, BLK), jnp.float32))
    grad_centres = totals[:, 0:3].reshape(SLABS, SLAB_BLOCKS, 3, BLK)
    grad_tangents = totals[:, 3:6].reshape(SLABS, SLAB_BLOCKS, 3, BLK)
    return grad_centres, grad_tangents
```

```python
import functools
import math

import jax
import jax.numpy as jnp
from jax import lax
from jax.experimental import pallas as pl
from jax.experimental.pallas import tpu as pltpu
from jax.sharding import PartitionSpec as P

REACH = 2
WIDTH_SQUARE = 4.0
SCALE = math.sqrt(2.0 * math.log2(math.e) / WIDTH_SQUARE)
F32, BF16 = jnp.float32, jnp.bfloat16
MESH = pl.DeviceIdType.MESH
TILE = 256
MOVES = [(ds, dc) for ds in (0, -1, 1) for dc in (0, -1, 1) if (ds, dc) != (0, 0)]


def region(level, side, blocks):
    extent = blocks + 2 * REACH
    first = (level + 1) * extent
    if side < 0:
        return first, REACH
    if side > 0:
        return first + REACH + blocks, REACH
    return first + REACH, blocks


def gather_kernel(blocks, slots, cen, tan, wts, cnt, prs, pcn, win, meta, send_sem, recv_sem):
    cells, slabs = lax.axis_size("cells"), lax.axis_size("slab")
    c, s = lax.axis_index("cells"), lax.axis_index("slab")
    segments = win.shape[2]
    peers = [
        {"slab": lax.rem(s + ds + slabs, slabs), "cells": lax.rem(c + dc + cells, cells)}
        for ds, dc in MOVES
    ]
    barrier = pltpu.get_barrier_semaphore()
    for peer in peers:
        pl.semaphore_signal(barrier, inc=1, device_id=peer, device_id_type=MESH)
    extent = blocks + 2 * REACH
    own = extent + REACH
    lane = lax.broadcasted_iota(jnp.int32, (1, segments), 1)
    table = jnp.zeros((1, segments), jnp.int32)
    for k in range(slots):
        table = jnp.where(lane == k, prs[0, k, 0], table)
        table = jnp.where(lane == slots + k, prs[0, k, 1], table)
    table = jnp.where(lane == 2 * slots, pcn[0, 0], table)
    for b in range(blocks):
        win[own + b, 0:3, :] = cen[0, b]
        win[own + b, 3:6, :] = tan[0, b]
        win[own + b, 6:7, :] = jnp.where(lane < cnt[0, b], wts[0, b : b + 1, :], 0.0)
        row = jnp.where(lane == 2 * slots + 1, cnt[0, b], table)
        win[own + b, 7:8, :] = row.astype(F32)
    pl.semaphore_wait(barrier, len(MOVES))
    copies = []
    for n, (ds, dc) in enumerate(MOVES):
        target, count = region(-ds, -dc, blocks)
        source = own + (blocks - REACH if dc > 0 else 0)
        copy = pltpu.make_async_remote_copy(
            src_ref=win.at[pl.ds(source, count)],
            dst_ref=win.at[pl.ds(target, count)],
            send_sem=send_sem.at[n],
            recv_sem=recv_sem.at[n],
            device_id=peers[n],
            device_id_type=MESH,
        )
        copy.start()
        copies.append(copy)
    for copy in copies:
        copy.wait()
    for slot in range(3 * extent):
        meta[slot : slot + 1, :] = win[slot, 7:8, 0:128].astype(jnp.int32)
    meta[3 * extent : 3 * extent + 8, :] = jnp.full((8, 128), c, jnp.int32)


def pieces(value):
    high = value.astype(BF16).astype(F32)
    rest = value - high
    middle = rest.astype(BF16).astype(F32)
    return high, middle, rest - middle


def spread(tile, row):
    return jnp.broadcast_to(tile[row : row + 1], tile.shape)


def position_rows(tile, norm_row, one_row):
    row = lax.broadcasted_iota(jnp.int32, tile.shape, 0)
    x, y, z = [spread(tile, r) * SCALE for r in range(3)]
    norm = -0.5 * (x * x + y * y + z * z)
    base = jnp.where(row < 3, tile * SCALE, 0.0)
    return jnp.where(row == norm_row, norm, jnp.where(row == one_row, 1.0, base))


def tangent_products(tile):
    row = lax.broadcasted_iota(jnp.int32, tile.shape, 0)
    t0, t1, t2 = [spread(tile, r) for r in range(3, 6)]
    left = jnp.where(row < 3, t0, jnp.where(row < 5, t1, t2))
    right = jnp.where(row == 0, t0, jnp.where((row == 1) | (row == 3), t1, t2))
    return left * right, row


def prepare_own(win, slot, vr, p):
    p1, p2, p3 = pieces(position_rows(win[slot], 4, 3))
    vr[p] = jnp.concatenate([p1, p2, p1, p2, p3, p1, p3, p2], axis=0).astype(BF16)


def prepare_unit(win, slot, start, ut, ft):
    tile = win[slot, :, pl.ds(start, TILE)]
    q1, q2, q3 = pieces(position_rows(tile, 3, 4))
    ut[...] = jnp.concatenate([q1, q1, q2, q2, q1, q3, q2, q3], axis=0).T.astype(BF16)
    products, row = tangent_products(tile)
    base = jnp.where(row < 6, spread(tile, 6) * products, 0.0)
    terms = jnp.concatenate([base] + [base * spread(tile, k) for k in range(3)], axis=0)
    ft[...] = jnp.concatenate(pieces(terms), axis=0).astype(BF16)


def dot(a, b):
    return lax.dot_general(a, b, (((1,), (0,)), ((), ())), preferred_element_type=F32)


def gauss_step(ut, vr, p, high, low, cols):
    gauss = jnp.exp2(dot(ut[...], vr[p, :, cols]))
    top = gauss.astype(BF16)
    high[:, cols] = top
    low[:, cols] = (gauss - top.astype(F32)).astype(BF16)


def sum_step(ft, high, low, acc, p, cols):
    whole = dot(ft[...], high[:, cols])
    part = dot(ft[0:32], low[:, cols])
    acc[p, :, cols] += whole[0:32] + whole[32:64] + whole[64:96] + part


def pair_kernel(
    blocks, slots, meta, win, gc, gt, acc, vr, ut0, ut1, f0, f1, h0, h1, l0, l1, units, counts
):
    segments = win.shape[2]
    extent = blocks + 2 * REACH
    own = extent + REACH
    chunks = segments // TILE
    cells = lax.axis_size("cells")
    slab_blocks = blocks * cells
    c = meta[3 * extent, 0]
    anchor = c * blocks - REACH
    low_own = c * blocks

    for p in range(blocks):
        counts[p] = 0

    def append(p, slot):
        at = counts[p]
        live = lax.div(meta[slot, 2 * slots + 1] + (TILE - 1), TILE)

        def one(k, carry):
            units[p, at + k] = slot * chunks + k
            return carry

        lax.fori_loop(0, live, one, 0)
        counts[p] = at + live

    def list_source(level, side):
        slot0 = region(level, side, blocks)[0]

        def one(k, carry):
            first = meta[slot0, k]
            second = meta[slot0, slots + k]
            upper = second >= slab_blocks
            if level == 0 and side == 0:
                inside = jnp.where(upper, second - slab_blocks, second)
                append(
                    first - low_own, jnp.where(upper, 2 * extent, extent) + inside - anchor
                )
            target = second - slab_blocks if level < 0 else second
            wanted = (target >= low_own) & (target < low_own + blocks)
            if level == 0:
                wanted = wanted & jnp.logical_not(upper)
            if level == 0 and side == 0:
                wanted = wanted & (first != second)

            @pl.when(wanted)
            def _():
                append(target - low_own, (level + 1) * extent + first - anchor)

            return carry

        lax.fori_loop(0, meta[slot0, 2 * slots], one, 0)

    list_source(0, 0)
    for side in (-1, 1):
        has = c > 0 if side < 0 else c < cells - 1
        pl.when(has)(functools.partial(list_source, 0, side))
        pl.when(has)(functools.partial(list_source, -1, side))
    list_source(-1, 0)

    acc[...] = jnp.zeros_like(acc)
    for p in range(blocks):
        prepare_own(win, own + p, vr, p)

    uts, fts, highs, lows = (ut0, ut1), (f0, f1), (h0, h1), (l0, l1)

    def run(width, p, total):
        step = 512 if width % 512 == 0 else 256

        def place(u):
            unit = units[p, u]
            return lax.div(unit, chunks), pl.multiple_of(lax.rem(unit, chunks) * TILE, TILE)

        def columns(i):
            return slice(i, i + step)

        prepare_unit(win, *place(0), uts[0], fts[0])
        for i in range(0, width, step):
            gauss_step(uts[0], vr, p, highs[0], lows[0], columns(i))
        prepare_unit(win, *place(1), uts[1], fts[1])

        def half(k, u):
            n = 1 - k
            for i in range(0, width, step):
                gauss_step(uts[n], vr, p, highs[n], lows[n], columns(i))
                sum_step(fts[k], highs[k], lows[k], acc, p, columns(i))
            prepare_unit(win, *place(u + 2), uts[k], fts[k])

        def body(m, carry):
            half(0, 2 * m)
            pl.when(2 * m + 1 < total)(functools.partial(half, 1, 2 * m + 1))
            return carry

        lax.fori_loop(0, lax.div(total + 1, 2), body, 0)

    def one_block(p, carry):
        total = counts[p]
        for k in range(2):
            units[p, total + k] = (own + p) * chunks
        width = lax.div(meta[own + p, 2 * slots + 1] + (TILE - 1), TILE)
        for k in range(1, chunks + 1):
            pl.when((width == k) & (total > 0))(functools.partial(run, k * TILE, p, total))
        return carry

    lax.fori_loop(0, blocks, one_block, 0)

    loss_scale = segments**-0.5
    for p in range(blocks):
        tile = win[own + p]
        products, row = tangent_products(tile)
        twice = jnp.where((row == 0) | (row == 3) | (row == 5), 1.0, 2.0)
        forms = jnp.where(row < 6, products * twice, 0.0)
        total = acc[p]
        weight = tile[6:7]
        sums = [
            jnp.sum(forms * total[8 * k : 8 * k + 8], axis=0, keepdims=True) for k in range(4)
        ]
        pull = (-4.0 * loss_scale / WIDTH_SQUARE) * weight
        gc[0, p] = jnp.concatenate(
            [pull * (tile[k : k + 1] * sums[0] - sums[k + 1]) for k in range(3)], axis=0
        )
        m = [total[k : k + 1] for k in range(6)]
        t = [tile[k : k + 1] for k in range(3, 6)]
        turn = (4.0 * loss_scale) * weight
        gt[0, p] = jnp.concatenate(
            [
                turn * (m[0] * t[0] + m[1] * t[1] + m[2] * t[2]),
                turn * (m[1] * t[0] + m[3] * t[1] + m[4] * t[2]),
                turn * (m[2] * t[0] + m[4] * t[1] + m[5] * t[2]),
            ],
            axis=0,
        )


def per_device(centres, tangents, weights, segment_count, pairs, pair_count):
    blocks, segments, slots = centres.shape[1], centres.shape[3], pairs.shape[1]
    extent = blocks + 2 * REACH
    vmem = pl.BlockSpec(memory_space=pltpu.VMEM)
    smem = pl.BlockSpec(memory_space=pltpu.SMEM)
    window, meta = pl.pallas_call(
        functools.partial(gather_kernel, blocks, slots),
        out_shape=(
            jax.ShapeDtypeStruct((3 * extent, 8, segments), F32),
            jax.ShapeDtypeStruct((3 * extent + 8, 128), jnp.int32),
        ),
        in_specs=[vmem, vmem, vmem, smem, smem, smem],
        out_specs=(vmem, vmem),
        scratch_shapes=[
            pltpu.SemaphoreType.DMA((len(MOVES),)),
            pltpu.SemaphoreType.DMA((len(MOVES),)),
        ],
        compiler_params=pltpu.CompilerParams(collective_id=0, has_side_effects=True),
        name="gather_window",
    )(centres, tangents, weights, segment_count, pairs, pair_count)
    most = (2 * REACH + 1) * 3 * (segments // TILE) + 4
    return pl.pallas_call(
        functools.partial(pair_kernel, blocks, slots),
        out_shape=(
            jax.ShapeDtypeStruct((1, blocks, 3, segments), F32),
            jax.ShapeDtypeStruct((1, blocks, 3, segments), F32),
        ),
        in_specs=[smem, vmem],
        out_specs=(vmem, vmem),
        scratch_shapes=[
            pltpu.VMEM((blocks, 32, segments), F32),
            pltpu.VMEM((blocks, 64, segments), BF16),
            pltpu.VMEM((TILE, 64), BF16),
            pltpu.VMEM((TILE, 64), BF16),
            pltpu.VMEM((96, TILE), BF16),
            pltpu.VMEM((96, TILE), BF16),
            pltpu.VMEM((TILE, segments), BF16),
            pltpu.VMEM((TILE, segments), BF16),
            pltpu.VMEM((TILE, segments), BF16),
            pltpu.VMEM((TILE, segments), BF16),
            pltpu.SMEM((blocks, most), jnp.int32),
            pltpu.SMEM((blocks,), jnp.int32),
        ],
        compiler_params=pltpu.CompilerParams(vmem_limit_bytes=32 << 20),
        name="pair_sums",
    )(meta, window)


def solution(mesh):
    placed = (
        P("slab", "cells", None, None),
        P("slab", "cells", None, None),
        P("slab", "cells", None),
        P("slab", "cells"),
        P("slab", "cells", None),
        P("slab", "cells"),
    )
    return jax.shard_map(
        per_device,
        mesh=mesh,
        in_specs=placed,
        out_specs=(P("slab", "cells", None, None), P("slab", "cells", None, None)),
        check_vma=False,
    )
```

```python
import functools
import math

import jax
import jax.numpy as jnp
from jax import lax
from jax.experimental import pallas as pl
from jax.experimental.pallas import tpu as pltpu
from jax.sharding import PartitionSpec as P

REACH = 2
WIDTH_SQUARE = 4.0
SCALE = math.sqrt(2.0 * math.log2(math.e) / WIDTH_SQUARE)
F32, BF16 = jnp.float32, jnp.bfloat16
MESH = pl.DeviceIdType.MESH
TILE = 256
MOVES = [(ds, dc) for ds in (0, -1, 1) for dc in (0, -1, 1) if (ds, dc) != (0, 0)]


def region(level, side, blocks):
    extent = blocks + 2 * REACH
    first = (level + 1) * extent
    if side < 0:
        return first, REACH
    if side > 0:
        return first + REACH + blocks, REACH
    return first + REACH, blocks


def gather_kernel(blocks, slots, cen, tan, wts, cnt, prs, pcn, win, meta, send_sem, recv_sem):
    cells, slabs = lax.axis_size("cells"), lax.axis_size("slab")
    c, s = lax.axis_index("cells"), lax.axis_index("slab")
    segments = win.shape[2]
    peers = [
        {"slab": lax.rem(s + ds + slabs, slabs), "cells": lax.rem(c + dc + cells, cells)}
        for ds, dc in MOVES
    ]
    barrier = pltpu.get_barrier_semaphore()
    for peer in peers:
        pl.semaphore_signal(barrier, inc=1, device_id=peer, device_id_type=MESH)
    extent = blocks + 2 * REACH
    own = extent + REACH
    lane = lax.broadcasted_iota(jnp.int32, (1, segments), 1)
    table = jnp.zeros((1, segments), jnp.int32)
    for k in range(slots):
        table = jnp.where(lane == k, prs[0, k], table)
        table = jnp.where(lane == slots + k, prs[1, k], table)
    table = jnp.where(lane == 2 * slots, pcn[0, 0], table)
    for b in range(blocks):
        for k in range(3):
            win[own + b, k : k + 1, :] = cen[k, b : b + 1, :]
            win[own + b, 3 + k : 4 + k, :] = tan[k, b : b + 1, :]
        win[own + b, 6:7, :] = jnp.where(lane < cnt[0, b], wts[0, b : b + 1, :], 0.0)
        row = jnp.where(lane == 2 * slots + 1, cnt[0, b], table)
        win[own + b, 7:8, :] = row.astype(F32)
    pl.semaphore_wait(barrier, len(MOVES))
    copies = []
    for n, (ds, dc) in enumerate(MOVES):
        target, count = region(-ds, -dc, blocks)
        source = own + (blocks - REACH if dc > 0 else 0)
        copy = pltpu.make_async_remote_copy(
            src_ref=win.at[pl.ds(source, count)],
            dst_ref=win.at[pl.ds(target, count)],
            send_sem=send_sem.at[n],
            recv_sem=recv_sem.at[n],
            device_id=peers[n],
            device_id_type=MESH,
        )
        copy.start()
        copies.append(copy)
    for copy in copies:
        copy.wait()
    for slot in range(3 * extent):
        meta[slot : slot + 1, :] = win[slot, 7:8, 0:128].astype(jnp.int32)
    meta[3 * extent : 3 * extent + 8, :] = jnp.full((8, 128), c, jnp.int32)


def pieces(value):
    high = value.astype(BF16).astype(F32)
    rest = value - high
    middle = rest.astype(BF16).astype(F32)
    return high, middle, rest - middle


def spread(tile, row):
    return jnp.broadcast_to(tile[row : row + 1], tile.shape)


def position_rows(tile, norm_row, one_row):
    row = lax.broadcasted_iota(jnp.int32, tile.shape, 0)
    x, y, z = [spread(tile, r) * SCALE for r in range(3)]
    norm = -0.5 * (x * x + y * y + z * z)
    base = jnp.where(row < 3, tile * SCALE, 0.0)
    return jnp.where(row == norm_row, norm, jnp.where(row == one_row, 1.0, base))


def tangent_products(tile):
    row = lax.broadcasted_iota(jnp.int32, tile.shape, 0)
    t0, t1, t2 = [spread(tile, r) for r in range(3, 6)]
    left = jnp.where(row < 3, t0, jnp.where(row < 5, t1, t2))
    right = jnp.where(row == 0, t0, jnp.where((row == 1) | (row == 3), t1, t2))
    return left * right, row


def prepare_own(win, slot, vr, p):
    p1, p2, p3 = pieces(position_rows(win[slot], 4, 3))
    vr[p] = jnp.concatenate([p1, p2, p1, p2, p3, p1, p3, p2], axis=0).astype(BF16)


def prepare_unit(win, slot, start, ut, ft):
    tile = win[slot, :, pl.ds(start, TILE)]
    q1, q2, q3 = pieces(position_rows(tile, 3, 4))
    ut[...] = jnp.concatenate([q1, q1, q2, q2, q1, q3, q2, q3], axis=0).T.astype(BF16)
    products, row = tangent_products(tile)
    base = jnp.where(row < 6, spread(tile, 6) * products, 0.0)
    terms = jnp.concatenate([base] + [base * spread(tile, k) for k in range(3)], axis=0)
    ft[...] = jnp.concatenate(pieces(terms), axis=0).astype(BF16)


def dot(a, b):
    return lax.dot_general(a, b, (((1,), (0,)), ((), ())), preferred_element_type=F32)


def gauss_step(ut, vr, p, high, low, cols):
    gauss = jnp.exp2(dot(ut[...], vr[p, :, cols]))
    top = gauss.astype(BF16)
    high[:, cols] = top
    low[:, cols] = (gauss - top.astype(F32)).astype(BF16)


def sum_step(ft, high, low, acc, p, cols):
    whole = dot(ft[...], high[:, cols])
    part = dot(ft[0:32], low[:, cols])
    acc[p, :, cols] += whole[0:32] + whole[32:64] + whole[64:96] + part


def pair_kernel(
    blocks, slots, meta_hbm, win_hbm, gc, gt, win, acc, vr, ut0, ut1, f0, f1, h0, h1, l0, l1,
    meta, units, counts, sems,
):
    table_copy = pltpu.make_async_copy(meta_hbm, meta, sems.at[0])
    window_copy = pltpu.make_async_copy(win_hbm, win, sems.at[1])
    table_copy.start()
    window_copy.start()
    acc[...] = jnp.zeros_like(acc)
    table_copy.wait()
    segments = win.shape[2]
    extent = blocks + 2 * REACH
    own = extent + REACH
    chunks = segments // TILE
    cells = lax.axis_size("cells")
    slab_blocks = blocks * cells
    c = meta[3 * extent, 0]
    anchor = c * blocks - REACH
    low_own = c * blocks

    for p in range(blocks):
        counts[p] = 0

    def append(p, slot):
        at = counts[p]
        live = lax.div(meta[slot, 2 * slots + 1] + (TILE - 1), TILE)

        def one(k, carry):
            units[p, at + k] = slot * chunks + k
            return carry

        lax.fori_loop(0, live, one, 0)
        counts[p] = at + live

    def list_source(level, side):
        slot0 = region(level, side, blocks)[0]

        def one(k, carry):
            first = meta[slot0, k]
            second = meta[slot0, slots + k]
            upper = second >= slab_blocks
            if level == 0 and side == 0:
                inside = jnp.where(upper, second - slab_blocks, second)
                append(
                    first - low_own, jnp.where(upper, 2 * extent, extent) + inside - anchor
                )
            target = second - slab_blocks if level < 0 else second
            wanted = (target >= low_own) & (target < low_own + blocks)
            if level == 0:
                wanted = wanted & jnp.logical_not(upper)
            if level == 0 and side == 0:
                wanted = wanted & (first != second)

            @pl.when(wanted)
            def _():
                append(target - low_own, (level + 1) * extent + first - anchor)

            return carry

        lax.fori_loop(0, meta[slot0, 2 * slots], one, 0)

    list_source(0, 0)
    for side in (-1, 1):
        has = c > 0 if side < 0 else c < cells - 1
        pl.when(has)(functools.partial(list_source, 0, side))
        pl.when(has)(functools.partial(list_source, -1, side))
    list_source(-1, 0)

    window_copy.wait()
    for p in range(blocks):
        prepare_own(win, own + p, vr, p)

    uts, fts, highs, lows = (ut0, ut1), (f0, f1), (h0, h1), (l0, l1)

    def run(width, p, total):
        step = 512 if width % 512 == 0 else 256

        def place(u):
            unit = units[p, u]
            return lax.div(unit, chunks), pl.multiple_of(lax.rem(unit, chunks) * TILE, TILE)

        def columns(i):
            return slice(i, i + step)

        prepare_unit(win, *place(0), uts[0], fts[0])
        for i in range(0, width, step):
            gauss_step(uts[0], vr, p, highs[0], lows[0], columns(i))
        prepare_unit(win, *place(1), uts[1], fts[1])

        def half(k, u):
            n = 1 - k
            for i in range(0, width, step):
                gauss_step(uts[n], vr, p, highs[n], lows[n], columns(i))
                sum_step(fts[k], highs[k], lows[k], acc, p, columns(i))
            prepare_unit(win, *place(u + 2), uts[k], fts[k])

        def body(m, carry):
            half(0, 2 * m)
            pl.when(2 * m + 1 < total)(functools.partial(half, 1, 2 * m + 1))
            return carry

        lax.fori_loop(0, lax.div(total + 1, 2), body, 0)

    def one_block(p, carry):
        total = counts[p]
        for k in range(2):
            units[p, total + k] = (own + p) * chunks
        width = lax.div(meta[own + p, 2 * slots + 1] + (TILE - 1), TILE)
        for k in range(1, chunks + 1):
            pl.when((width == k) & (total > 0))(functools.partial(run, k * TILE, p, total))
        return carry

    lax.fori_loop(0, blocks, one_block, 0)

    loss_scale = segments**-0.5
    for p in range(blocks):
        tile = win[own + p]
        products, row = tangent_products(tile)
        twice = jnp.where((row == 0) | (row == 3) | (row == 5), 1.0, 2.0)
        forms = jnp.where(row < 6, products * twice, 0.0)
        total = acc[p]
        weight = tile[6:7]
        sums = [
            jnp.sum(forms * total[8 * k : 8 * k + 8], axis=0, keepdims=True) for k in range(4)
        ]
        pull = (-4.0 * loss_scale / WIDTH_SQUARE) * weight
        for k in range(3):
            gc[k, p : p + 1, :] = pull * (tile[k : k + 1] * sums[0] - sums[k + 1])
        m = [total[k : k + 1] for k in range(6)]
        t = [tile[k : k + 1] for k in range(3, 6)]
        turn = (4.0 * loss_scale) * weight
        for k, (x, y, z) in enumerate(((0, 1, 2), (1, 3, 4), (2, 4, 5))):
            gt[k, p : p + 1, :] = turn * (m[x] * t[0] + m[y] * t[1] + m[z] * t[2])


def per_device(centres, tangents, weights, segment_count, pairs, pair_count):
    blocks, segments, slots = centres.shape[1], centres.shape[3], pairs.shape[1]
    extent = blocks + 2 * REACH
    vmem = pl.BlockSpec(memory_space=pltpu.VMEM)
    smem = pl.BlockSpec(memory_space=pltpu.SMEM)
    window, meta = pl.pallas_call(
        functools.partial(gather_kernel, blocks, slots),
        out_shape=(
            jax.ShapeDtypeStruct((3 * extent, 8, segments), F32),
            jax.ShapeDtypeStruct((3 * extent + 8, 128), jnp.int32),
        ),
        in_specs=[vmem, vmem, vmem, smem, smem, smem],
        out_specs=(vmem, vmem),
        scratch_shapes=[
            pltpu.SemaphoreType.DMA((len(MOVES),)),
            pltpu.SemaphoreType.DMA((len(MOVES),)),
        ],
        compiler_params=pltpu.CompilerParams(collective_id=0, has_side_effects=True),
        name="gather_window",
    )(
        jnp.transpose(centres[0], (1, 0, 2)),
        jnp.transpose(tangents[0], (1, 0, 2)),
        weights,
        segment_count,
        jnp.transpose(pairs[0]),
        pair_count,
    )
    most = (2 * REACH + 1) * 3 * (segments // TILE) + 4
    hbm = pl.BlockSpec(memory_space=pltpu.HBM)
    grads = pl.pallas_call(
        functools.partial(pair_kernel, blocks, slots),
        out_shape=(
            jax.ShapeDtypeStruct((3, blocks, segments), F32),
            jax.ShapeDtypeStruct((3, blocks, segments), F32),
        ),
        in_specs=[hbm, hbm],
        out_specs=(vmem, vmem),
        scratch_shapes=[
            pltpu.VMEM((3 * extent, 8, segments), F32),
            pltpu.VMEM((blocks, 32, segments), F32),
            pltpu.VMEM((blocks, 64, segments), BF16),
            pltpu.VMEM((TILE, 64), BF16),
            pltpu.VMEM((TILE, 64), BF16),
            pltpu.VMEM((96, TILE), BF16),
            pltpu.VMEM((96, TILE), BF16),
            pltpu.VMEM((TILE, segments), BF16),
            pltpu.VMEM((TILE, segments), BF16),
            pltpu.VMEM((TILE, segments), BF16),
            pltpu.VMEM((TILE, segments), BF16),
            pltpu.SMEM((3 * extent + 8, 128), jnp.int32),
            pltpu.SMEM((blocks, most), jnp.int32),
            pltpu.SMEM((blocks,), jnp.int32),
            pltpu.SemaphoreType.DMA((2,)),
        ],
        compiler_params=pltpu.CompilerParams(vmem_limit_bytes=60 << 20),
        name="pair_sums",
    )(meta, window)
    return tuple(jnp.transpose(grad, (1, 0, 2))[None] for grad in grads)


def solution(mesh):
    placed = (
        P("slab", "cells", None, None),
        P("slab", "cells", None, None),
        P("slab", "cells", None),
        P("slab", "cells"),
        P("slab", "cells", None),
        P("slab", "cells"),
    )
    return jax.shard_map(
        per_device,
        mesh=mesh,
        in_specs=placed,
        out_specs=(P("slab", "cells", None, None), P("slab", "cells", None, None)),
        check_vma=False,
    )
```

```python
import functools
import math

import jax
import jax.numpy as jnp
from jax import lax
from jax.experimental import pallas as pl
from jax.experimental.pallas import tpu as pltpu
from jax.sharding import PartitionSpec as P

REACH = 2
WIDTH_SQUARE = 4.0
SCALE = math.sqrt(2.0 * math.log2(math.e) / WIDTH_SQUARE)
F32, BF16 = jnp.float32, jnp.bfloat16
MESH = pl.DeviceIdType.MESH
TILE = 128
GROUP = 4
STRIP = 256
MOVES = [(ds, dc) for ds in (0, -1, 1) for dc in (0, -1, 1) if (ds, dc) != (0, 0)]


def region(level, side, blocks):
    extent = blocks + 2 * REACH
    first = (level + 1) * extent
    if side < 0:
        return first, REACH
    if side > 0:
        return first + REACH + blocks, REACH
    return first + REACH, blocks


def gather_kernel(blocks, slots, cen, tan, wts, cnt, prs, pcn, win, meta, send_sem, recv_sem):
    cells, slabs = lax.axis_size("cells"), lax.axis_size("slab")
    c, s = lax.axis_index("cells"), lax.axis_index("slab")
    segments = win.shape[2]
    peers = [
        {"slab": lax.rem(s + ds + slabs, slabs), "cells": lax.rem(c + dc + cells, cells)}
        for ds, dc in MOVES
    ]
    barrier = pltpu.get_barrier_semaphore()
    for peer in peers:
        pl.semaphore_signal(barrier, inc=1, device_id=peer, device_id_type=MESH)
    extent = blocks + 2 * REACH
    own = extent + REACH
    lane = lax.broadcasted_iota(jnp.int32, (1, segments), 1)
    table = jnp.zeros((1, segments), jnp.int32)
    for k in range(slots):
        table = jnp.where(lane == k, prs[0, k], table)
        table = jnp.where(lane == slots + k, prs[1, k], table)
    table = jnp.where(lane == 2 * slots, pcn[0, 0], table)
    for b in range(blocks):
        for k in range(3):
            win[own + b, k : k + 1, :] = cen[k, b : b + 1, :]
            win[own + b, 3 + k : 4 + k, :] = tan[k, b : b + 1, :]
        win[own + b, 6:7, :] = jnp.where(lane < cnt[0, b], wts[0, b : b + 1, :], 0.0)
        row = jnp.where(lane == 2 * slots + 1, cnt[0, b], table)
        win[own + b, 7:8, :] = row.astype(F32)
    pl.semaphore_wait(barrier, len(MOVES))
    copies = []
    for n, (ds, dc) in enumerate(MOVES):
        target, count = region(-ds, -dc, blocks)
        source = own + (blocks - REACH if dc > 0 else 0)
        copy = pltpu.make_async_remote_copy(
            src_ref=win.at[pl.ds(source, count)],
            dst_ref=win.at[pl.ds(target, count)],
            send_sem=send_sem.at[n],
            recv_sem=recv_sem.at[n],
            device_id=peers[n],
            device_id_type=MESH,
        )
        copy.start()
        copies.append(copy)
    for copy in copies:
        copy.wait()
    for slot in range(3 * extent):
        meta[slot : slot + 1, :] = win[slot, 7:8, 0:128].astype(jnp.int32)
    meta[3 * extent : 3 * extent + 8, :] = jnp.full((8, 128), c, jnp.int32)


def pieces(value):
    high = value.astype(BF16).astype(F32)
    rest = value - high
    middle = rest.astype(BF16).astype(F32)
    return high, middle, rest - middle


def spread(tile, row):
    return jnp.broadcast_to(tile[row : row + 1], tile.shape)


def position_rows(tile, norm_row, one_row):
    row = lax.broadcasted_iota(jnp.int32, tile.shape, 0)
    x, y, z = [spread(tile, r) * SCALE for r in range(3)]
    norm = -0.5 * (x * x + y * y + z * z)
    base = jnp.where(row < 3, tile * SCALE, 0.0)
    return jnp.where(row == norm_row, norm, jnp.where(row == one_row, 1.0, base))


def tangent_products(tile):
    row = lax.broadcasted_iota(jnp.int32, tile.shape, 0)
    t0, t1, t2 = [spread(tile, r) for r in range(3, 6)]
    left = jnp.where(row < 3, t0, jnp.where(row < 5, t1, t2))
    right = jnp.where(row == 0, t0, jnp.where((row == 1) | (row == 3), t1, t2))
    return left * right, row


def prepare_own(win, slot, vr, p):
    p1, p2, p3 = pieces(position_rows(win[slot], 4, 3))
    vr[p] = jnp.concatenate([p1, p2, p1, p2, p3, p1, p3, p2], axis=0).astype(BF16)


def prepare_unit(win, places, ut, ft):
    tile = jnp.concatenate([win[slot, :, pl.ds(start, TILE)] for slot, start in places], axis=1)
    q1, q2, q3 = pieces(position_rows(tile, 3, 4))
    ut[...] = jnp.concatenate([q1, q1, q2, q2, q1, q3, q2, q3], axis=0).T.astype(BF16)
    products, row = tangent_products(tile)
    base = jnp.where(row < 6, spread(tile, 6) * products, 0.0)
    terms = jnp.concatenate([base] + [base * spread(tile, k) for k in range(3)], axis=0)
    ft[...] = jnp.concatenate(pieces(terms), axis=0).astype(BF16)


def dot(a, b):
    return lax.dot_general(a, b, (((1,), (0,)), ((), ())), preferred_element_type=F32)


def gauss_step(ut, vr, p, high, low, cols):
    gauss = jnp.exp2(dot(ut[...], vr[p, :, cols]))
    top = gauss.astype(BF16)
    high[:, cols] = top
    low[:, cols] = (gauss - top.astype(F32)).astype(BF16)


def sum_step(ft, high, low, acc, p, cols):
    whole = dot(ft[...], high[:, cols])
    part = dot(ft[0:32], low[:, cols])
    acc[p, :, cols] += whole[0:32] + whole[32:64] + whole[64:96] + part


def pair_kernel(
    blocks, slots, meta_hbm, win_hbm, gc, gt, win, acc, vr, ut0, ut1, f0, f1, h0, h1, l0, l1,
    meta, units, counts, sems,
):
    table_copy = pltpu.make_async_copy(meta_hbm, meta, sems.at[0])
    window_copy = pltpu.make_async_copy(
        win_hbm, win.at[pl.ds(0, win_hbm.shape[0])], sems.at[1]
    )
    table_copy.start()
    window_copy.start()
    acc[...] = jnp.zeros_like(acc)
    win[win_hbm.shape[0]] = jnp.zeros(win.shape[1:], F32)
    table_copy.wait()
    segments = win.shape[2]
    extent = blocks + 2 * REACH
    own = extent + REACH
    chunks = segments // TILE
    cells = lax.axis_size("cells")
    slab_blocks = blocks * cells
    c = meta[3 * extent, 0]
    anchor = c * blocks - REACH
    low_own = c * blocks

    for p in range(blocks):
        counts[p] = 0

    def append(p, slot):
        at = counts[p]
        live = lax.div(meta[slot, 2 * slots + 1] + (TILE - 1), TILE)

        for k in range(chunks):
            units[p, at + k] = slot * chunks + k
        counts[p] = at + live

    def list_source(level, side):
        slot0 = region(level, side, blocks)[0]

        def one(k, carry):
            first = meta[slot0, k]
            second = meta[slot0, slots + k]
            upper = second >= slab_blocks
            if level == 0 and side == 0:
                inside = jnp.where(upper, second - slab_blocks, second)
                append(
                    first - low_own, jnp.where(upper, 2 * extent, extent) + inside - anchor
                )
            target = second - slab_blocks if level < 0 else second
            wanted = (target >= low_own) & (target < low_own + blocks)
            if level == 0:
                wanted = wanted & jnp.logical_not(upper)
            if level == 0 and side == 0:
                wanted = wanted & (first != second)

            @pl.when(wanted)
            def _():
                append(target - low_own, (level + 1) * extent + first - anchor)

            return carry

        lax.fori_loop(0, meta[slot0, 2 * slots], one, 0)

    list_source(0, 0)
    for side in (-1, 1):
        has = c > 0 if side < 0 else c < cells - 1
        pl.when(has)(functools.partial(list_source, 0, side))
        pl.when(has)(functools.partial(list_source, -1, side))
    list_source(-1, 0)

    window_copy.wait()
    for p in range(blocks):
        prepare_own(win, own + p, vr, p)

    uts, fts, highs, lows = (ut0, ut1), (f0, f1), (h0, h1), (l0, l1)

    def run(width, p, total):
        strips = [slice(i, min(i + STRIP, width)) for i in range(0, width, STRIP)]

        def places(u):
            found = []
            for k in range(GROUP):
                unit = units[p, GROUP * u + k]
                start = pl.multiple_of(lax.rem(unit, chunks) * TILE, TILE)
                found.append((lax.div(unit, chunks), start))
            return found

        prepare_unit(win, places(0), uts[0], fts[0])
        for cols in strips:
            gauss_step(uts[0], vr, p, highs[0], lows[0], cols)
        prepare_unit(win, places(1), uts[1], fts[1])

        def half(k, u):
            n = 1 - k
            for cols in strips:
                sum_step(fts[k], highs[k], lows[k], acc, p, cols)
                gauss_step(uts[n], vr, p, highs[n], lows[n], cols)
            prepare_unit(win, places(u + 2), uts[k], fts[k])

        def body(m, carry):
            half(0, 2 * m)
            pl.when(2 * m + 1 < total)(functools.partial(half, 1, 2 * m + 1))
            return carry

        lax.fori_loop(0, lax.div(total + 1, 2), body, 0)

    def one_block(p, carry):
        total = counts[p]
        for k in range(3 * GROUP):
            units[p, total + k] = 3 * extent * chunks
        width = lax.div(meta[own + p, 2 * slots + 1] + (TILE - 1), TILE)
        for k in range(chunks // 2, chunks + 1):
            pl.when((width == k) & (total > 0))(
                functools.partial(run, k * TILE, p, lax.div(total + GROUP - 1, GROUP))
            )
        return carry

    lax.fori_loop(0, blocks, one_block, 0)

    loss_scale = segments**-0.5
    for p in range(blocks):
        tile = win[own + p]
        products, row = tangent_products(tile)
        twice = jnp.where((row == 0) | (row == 3) | (row == 5), 1.0, 2.0)
        forms = jnp.where(row < 6, products * twice, 0.0)
        total = acc[p]
        weight = tile[6:7]
        sums = [
            jnp.sum(forms * total[8 * k : 8 * k + 8], axis=0, keepdims=True) for k in range(4)
        ]
        pull = (-4.0 * loss_scale / WIDTH_SQUARE) * weight
        for k in range(3):
            gc[k, p : p + 1, :] = pull * (tile[k : k + 1] * sums[0] - sums[k + 1])
        m = [total[k : k + 1] for k in range(6)]
        t = [tile[k : k + 1] for k in range(3, 6)]
        turn = (4.0 * loss_scale) * weight
        for k, (x, y, z) in enumerate(((0, 1, 2), (1, 3, 4), (2, 4, 5))):
            gt[k, p : p + 1, :] = turn * (m[x] * t[0] + m[y] * t[1] + m[z] * t[2])


def per_device(centres, tangents, weights, segment_count, pairs, pair_count):
    blocks, segments, slots = centres.shape[1], centres.shape[3], pairs.shape[1]
    extent = blocks + 2 * REACH
    vmem = pl.BlockSpec(memory_space=pltpu.VMEM)
    smem = pl.BlockSpec(memory_space=pltpu.SMEM)
    window, meta = pl.pallas_call(
        functools.partial(gather_kernel, blocks, slots),
        out_shape=(
            jax.ShapeDtypeStruct((3 * extent, 8, segments), F32),
            jax.ShapeDtypeStruct((3 * extent + 8, 128), jnp.int32),
        ),
        in_specs=[vmem, vmem, vmem, smem, smem, smem],
        out_specs=(vmem, vmem),
        scratch_shapes=[
            pltpu.SemaphoreType.DMA((len(MOVES),)),
            pltpu.SemaphoreType.DMA((len(MOVES),)),
        ],
        compiler_params=pltpu.CompilerParams(collective_id=0, has_side_effects=True),
        name="gather_window",
    )(
        jnp.transpose(centres[0], (1, 0, 2)),
        jnp.transpose(tangents[0], (1, 0, 2)),
        weights,
        segment_count,
        jnp.transpose(pairs[0]),
        pair_count,
    )
    most = (2 * REACH + 1) * 3 * (segments // TILE) + 3 * GROUP
    hbm = pl.BlockSpec(memory_space=pltpu.HBM)
    grads = pl.pallas_call(
        functools.partial(pair_kernel, blocks, slots),
        out_shape=(
            jax.ShapeDtypeStruct((3, blocks, segments), F32),
            jax.ShapeDtypeStruct((3, blocks, segments), F32),
        ),
        in_specs=[hbm, hbm],
        out_specs=(vmem, vmem),
        scratch_shapes=[
            pltpu.VMEM((3 * extent + 1, 8, segments), F32),
            pltpu.VMEM((blocks, 32, segments), F32),
            pltpu.VMEM((blocks, 64, segments), BF16),
            pltpu.VMEM((GROUP * TILE, 64), BF16),
            pltpu.VMEM((GROUP * TILE, 64), BF16),
            pltpu.VMEM((96, GROUP * TILE), BF16),
            pltpu.VMEM((96, GROUP * TILE), BF16),
            pltpu.VMEM((GROUP * TILE, segments), BF16),
            pltpu.VMEM((GROUP * TILE, segments), BF16),
            pltpu.VMEM((GROUP * TILE, segments), BF16),
            pltpu.VMEM((GROUP * TILE, segments), BF16),
            pltpu.SMEM((3 * extent + 8, 128), jnp.int32),
            pltpu.SMEM((blocks, most), jnp.int32),
            pltpu.SMEM((blocks,), jnp.int32),
            pltpu.SemaphoreType.DMA((2,)),
        ],
        compiler_params=pltpu.CompilerParams(vmem_limit_bytes=60 << 20),
        name="pair_sums",
    )(meta, window)
    return tuple(jnp.transpose(grad, (1, 0, 2))[None] for grad in grads)


def solution(mesh):
    placed = (
        P("slab", "cells", None, None),
        P("slab", "cells", None, None),
        P("slab", "cells", None),
        P("slab", "cells"),
        P("slab", "cells", None),
        P("slab", "cells"),
    )
    return jax.shard_map(
        per_device,
        mesh=mesh,
        in_specs=placed,
        out_specs=(P("slab", "cells", None, None), P("slab", "cells", None, None)),
        check_vma=False,
    )
```

```python
import functools
import math

import jax
import jax.numpy as jnp
from jax import lax
from jax.experimental import pallas as pl
from jax.experimental.pallas import tpu as pltpu
from jax.sharding import PartitionSpec as P

REACH = 2
WIDTH_SQUARE = 4.0
SCALE = math.sqrt(2.0 * math.log2(math.e) / WIDTH_SQUARE)
F32, BF16 = jnp.float32, jnp.bfloat16
MESH = pl.DeviceIdType.MESH
TILE = 128
GROUP = 4
STRIP = 256
SIDES = ((-1, 0), (1, 0), (0, -1), (0, 1))


def when(condition, action):
    pl.when(condition)(action)


def gather_kernel(blocks, slots, cen, tan, wts, cnt, prs, pcn, win, meta, send_sem, recv_sem):
    cells, slabs = lax.axis_size("cells"), lax.axis_size("slab")
    c, s = lax.axis_index("cells"), lax.axis_index("slab")
    segments = win.shape[2]
    extent = blocks + 2 * REACH
    own = extent + REACH
    there = {(-1, 0): s > 0, (1, 0): s < slabs - 1, (0, -1): c > 0, (0, 1): c < cells - 1}

    def device(ds, dc):
        return {
            "slab": lax.rem(s + ds + slabs, slabs),
            "cells": lax.rem(c + dc + cells, cells),
        }

    barrier = pltpu.get_barrier_semaphore()
    for side in SIDES:

        def greet(side=side):
            pl.semaphore_signal(
                barrier, inc=1, device_id=device(*side), device_id_type=MESH
            )

        when(there[side], greet)

    def clear(first, count):
        def store():
            win[pl.ds(first, count)] = jnp.zeros((count,) + win.shape[1:], F32)

        return store

    when(s == 0, clear(0, extent))
    when(s == slabs - 1, clear(2 * extent, extent))
    for level in range(3):
        when(c == 0, clear(level * extent, REACH))
        when(c == cells - 1, clear(level * extent + REACH + blocks, REACH))

    lane = lax.broadcasted_iota(jnp.int32, (1, segments), 1)
    table = jnp.zeros((1, segments), jnp.int32)
    for k in range(slots):
        table = jnp.where(lane == k, prs[0, k], table)
        table = jnp.where(lane == slots + k, prs[1, k], table)
    table = jnp.where(lane == 2 * slots, pcn[0, 0], table)
    for b in range(blocks):
        for k in range(3):
            win[own + b, k : k + 1, :] = cen[k, b : b + 1, :]
            win[own + b, 3 + k : 4 + k, :] = tan[k, b : b + 1, :]
        win[own + b, 6:7, :] = jnp.where(lane < cnt[0, b], wts[0, b : b + 1, :], 0.0)
        row = jnp.where(lane == 2 * slots + 1, cnt[0, b], table)
        win[own + b, 7:8, :] = row.astype(F32)
    pl.semaphore_wait(barrier, sum(there[side].astype(jnp.int32) for side in SIDES))

    used = iter(range(send_sem.shape[0]))

    def copy(source, target, count, side):
        n = next(used)
        return pltpu.make_async_remote_copy(
            src_ref=win.at[pl.ds(source, count)],
            dst_ref=win.at[pl.ds(target, count)],
            send_sem=send_sem.at[n],
            recv_sem=recv_sem.at[n],
            device_id=device(*side),
            device_id_type=MESH,
        )

    rims = {-1: 0, 1: blocks - REACH}
    halos = {-1: REACH + blocks, 1: 0}
    first_hop, second_hop = [], []
    for ds in (-1, 1):
        for dc in (-1, 1):
            block = rims[dc]
            one = copy(own + block, (1 - ds) * extent + REACH + block, REACH, (ds, 0))
            when(there[ds, 0], one.start)
            first_hop.append((ds, dc, one))
    beside = []
    for dc in (-1, 1):
        one = copy(own + rims[dc], extent + halos[dc], REACH, (0, dc))
        when(there[0, dc], one.start)
        beside.append((dc, one))
    for ds, dc, one in first_hop:
        came = there[-ds, 0]
        when(came, one.wait_recv)
        level = (1 - ds) * extent
        more = copy(level + REACH + rims[dc], level + halos[dc], REACH, (0, dc))
        when(came & there[0, dc], more.start)
        second_hop.append((came, dc, more))
    for ds, dc, one in first_hop:
        when(there[ds, 0], one.wait_send)
    for dc, one in beside:
        when(there[0, dc], one.wait_send)
        when(there[0, -dc], one.wait_recv)
    for came, dc, more in second_hop:
        when(came & there[0, dc], more.wait_send)
        when(came & there[0, -dc], more.wait_recv)
    for slot in range(3 * extent):
        meta[slot : slot + 1, :] = win[slot, 7:8, 0:128].astype(jnp.int32)
    meta[3 * extent : 3 * extent + 8, :] = jnp.full((8, 128), c, jnp.int32)


def pieces(value):
    high = value.astype(BF16).astype(F32)
    rest = value - high
    middle = rest.astype(BF16).astype(F32)
    return high, middle, rest - middle


def spread(tile, row):
    return jnp.broadcast_to(tile[row : row + 1], tile.shape)


def position_rows(tile, norm_row, one_row):
    row = lax.broadcasted_iota(jnp.int32, tile.shape, 0)
    x, y, z = [spread(tile, r) * SCALE for r in range(3)]
    norm = -0.5 * (x * x + y * y + z * z)
    base = jnp.where(row < 3, tile * SCALE, 0.0)
    return jnp.where(row == norm_row, norm, jnp.where(row == one_row, 1.0, base))


def tangent_products(tile):
    row = lax.broadcasted_iota(jnp.int32, tile.shape, 0)
    t0, t1, t2 = [spread(tile, r) for r in range(3, 6)]
    left = jnp.where(row < 3, t0, jnp.where(row < 5, t1, t2))
    right = jnp.where(row == 0, t0, jnp.where((row == 1) | (row == 3), t1, t2))
    return left * right, row


def prepare_own(win, slot, vr, p):
    p1, p2, p3 = pieces(position_rows(win[slot], 4, 3))
    vr[p] = jnp.concatenate([p1, p2, p1, p2, p3, p1, p3, p2], axis=0).astype(BF16)


def prepare_unit(win, places, ut, ft):
    tile = jnp.concatenate([win[slot, :, pl.ds(start, TILE)] for slot, start in places], axis=1)
    q1, q2, q3 = pieces(position_rows(tile, 3, 4))
    ut[...] = jnp.concatenate([q1, q1, q2, q2, q1, q3, q2, q3], axis=0).T.astype(BF16)
    products, row = tangent_products(tile)
    base = jnp.where(row < 6, spread(tile, 6) * products, 0.0)
    terms = jnp.concatenate([base] + [base * spread(tile, k) for k in range(3)], axis=0)
    ft[...] = jnp.concatenate(pieces(terms), axis=0).astype(BF16)


def dot(a, b):
    return lax.dot_general(a, b, (((1,), (0,)), ((), ())), preferred_element_type=F32)


def gauss_step(ut, vr, p, high, low, cols):
    gauss = jnp.exp2(dot(ut[...], vr[p, :, cols]))
    top = gauss.astype(BF16)
    high[:, cols] = top
    low[:, cols] = (gauss - top.astype(F32)).astype(BF16)


def sum_step(ft, high, low, acc, p, cols):
    whole = dot(ft[...], high[:, cols])
    part = dot(ft[0:32], low[:, cols])
    acc[p, :, cols] += whole[0:32] + whole[32:64] + whole[64:96] + part


def pair_kernel(
    blocks, slots, meta_hbm, win_hbm, gc, gt, win, acc, vr, ut0, ut1, f0, f1, h0, h1, l0, l1,
    meta, units, counts, sems,
):
    table_copy = pltpu.make_async_copy(meta_hbm, meta, sems.at[0])
    window_copy = pltpu.make_async_copy(
        win_hbm, win.at[pl.ds(0, win_hbm.shape[0])], sems.at[1]
    )
    table_copy.start()
    window_copy.start()
    acc[...] = jnp.zeros_like(acc)
    win[win_hbm.shape[0]] = jnp.zeros(win.shape[1:], F32)
    table_copy.wait()
    segments = win.shape[2]
    extent = blocks + 2 * REACH
    own = extent + REACH
    chunks = segments // TILE
    cells = lax.axis_size("cells")
    slab_blocks = blocks * cells
    c = meta[3 * extent, 0]
    anchor = c * blocks - REACH
    low_own = c * blocks

    for p in range(blocks):
        counts[p] = 0

    def append(p, slot):
        at = counts[p]
        live = lax.div(meta[slot, 2 * slots + 1] + (TILE - 1), TILE)

        for k in range(chunks):
            units[p, at + k] = slot * chunks + k
        counts[p] = at + live

    def list_source(level, side):
        slot0 = (level + 1) * extent + {-1: 0, 0: REACH, 1: REACH + blocks}[side]

        def one(k, carry):
            first = meta[slot0, k]
            second = meta[slot0, slots + k]
            upper = second >= slab_blocks
            if level == 0 and side == 0:
                inside = jnp.where(upper, second - slab_blocks, second)
                append(
                    first - low_own, jnp.where(upper, 2 * extent, extent) + inside - anchor
                )
            target = second - slab_blocks if level < 0 else second
            wanted = (target >= low_own) & (target < low_own + blocks)
            if level == 0:
                wanted = wanted & jnp.logical_not(upper)
            if level == 0 and side == 0:
                wanted = wanted & (first != second)

            @pl.when(wanted)
            def _():
                append(target - low_own, (level + 1) * extent + first - anchor)

            return carry

        lax.fori_loop(0, meta[slot0, 2 * slots], one, 0)

    list_source(0, 0)
    for side in (-1, 1):
        has = c > 0 if side < 0 else c < cells - 1
        pl.when(has)(functools.partial(list_source, 0, side))
        pl.when(has)(functools.partial(list_source, -1, side))
    list_source(-1, 0)

    window_copy.wait()
    for p in range(blocks):
        prepare_own(win, own + p, vr, p)

    uts, fts, highs, lows = (ut0, ut1), (f0, f1), (h0, h1), (l0, l1)

    def run(width, p, total):
        strips = [slice(i, min(i + STRIP, width)) for i in range(0, width, STRIP)]

        def places(u):
            found = []
            for k in range(GROUP):
                unit = units[p, GROUP * u + k]
                start = pl.multiple_of(lax.rem(unit, chunks) * TILE, TILE)
                found.append((lax.div(unit, chunks), start))
            return found

        prepare_unit(win, places(0), uts[0], fts[0])
        for cols in strips:
            gauss_step(uts[0], vr, p, highs[0], lows[0], cols)
        prepare_unit(win, places(1), uts[1], fts[1])

        def half(k, u):
            n = 1 - k
            for cols in strips:
                sum_step(fts[k], highs[k], lows[k], acc, p, cols)
                gauss_step(uts[n], vr, p, highs[n], lows[n], cols)
            prepare_unit(win, places(u + 2), uts[k], fts[k])

        def body(m, carry):
            half(0, 2 * m)
            pl.when(2 * m + 1 < total)(functools.partial(half, 1, 2 * m + 1))
            return carry

        lax.fori_loop(0, lax.div(total + 1, 2), body, 0)

    def one_block(p, carry):
        total = counts[p]
        for k in range(3 * GROUP):
            units[p, total + k] = 3 * extent * chunks
        width = lax.div(meta[own + p, 2 * slots + 1] + (TILE - 1), TILE)
        for k in range(chunks // 2, chunks + 1):
            pl.when((width == k) & (total > 0))(
                functools.partial(run, k * TILE, p, lax.div(total + GROUP - 1, GROUP))
            )
        return carry

    lax.fori_loop(0, blocks, one_block, 0)

    loss_scale = segments**-0.5
    for p in range(blocks):
        tile = win[own + p]
        products, row = tangent_products(tile)
        twice = jnp.where((row == 0) | (row == 3) | (row == 5), 1.0, 2.0)
        forms = jnp.where(row < 6, products * twice, 0.0)
        total = acc[p]
        weight = tile[6:7]
        sums = [
            jnp.sum(forms * total[8 * k : 8 * k + 8], axis=0, keepdims=True) for k in range(4)
        ]
        pull = (-4.0 * loss_scale / WIDTH_SQUARE) * weight
        for k in range(3):
            gc[k, p : p + 1, :] = pull * (tile[k : k + 1] * sums[0] - sums[k + 1])
        m = [total[k : k + 1] for k in range(6)]
        t = [tile[k : k + 1] for k in range(3, 6)]
        turn = (4.0 * loss_scale) * weight
        for k, (x, y, z) in enumerate(((0, 1, 2), (1, 3, 4), (2, 4, 5))):
            gt[k, p : p + 1, :] = turn * (m[x] * t[0] + m[y] * t[1] + m[z] * t[2])


def per_device(centres, tangents, weights, segment_count, pairs, pair_count):
    blocks, segments, slots = centres.shape[1], centres.shape[3], pairs.shape[1]
    extent = blocks + 2 * REACH
    vmem = pl.BlockSpec(memory_space=pltpu.VMEM)
    smem = pl.BlockSpec(memory_space=pltpu.SMEM)
    window, meta = pl.pallas_call(
        functools.partial(gather_kernel, blocks, slots),
        out_shape=(
            jax.ShapeDtypeStruct((3 * extent, 8, segments), F32),
            jax.ShapeDtypeStruct((3 * extent + 8, 128), jnp.int32),
        ),
        in_specs=[vmem, vmem, vmem, smem, smem, smem],
        out_specs=(vmem, vmem),
        scratch_shapes=[
            pltpu.SemaphoreType.DMA((10,)),
            pltpu.SemaphoreType.DMA((10,)),
        ],
        compiler_params=pltpu.CompilerParams(collective_id=0, has_side_effects=True),
        name="gather_window",
    )(
        jnp.transpose(centres[0], (1, 0, 2)),
        jnp.transpose(tangents[0], (1, 0, 2)),
        weights,
        segment_count,
        jnp.transpose(pairs[0]),
        pair_count,
    )
    most = (2 * REACH + 1) * 3 * (segments // TILE) + 3 * GROUP
    hbm = pl.BlockSpec(memory_space=pltpu.HBM)
    grads = pl.pallas_call(
        functools.partial(pair_kernel, blocks, slots),
        out_shape=(
            jax.ShapeDtypeStruct((3, blocks, segments), F32),
            jax.ShapeDtypeStruct((3, blocks, segments), F32),
        ),
        in_specs=[hbm, hbm],
        out_specs=(vmem, vmem),
        scratch_shapes=[
            pltpu.VMEM((3 * extent + 1, 8, segments), F32),
            pltpu.VMEM((blocks, 32, segments), F32),
            pltpu.VMEM((blocks, 64, segments), BF16),
            pltpu.VMEM((GROUP * TILE, 64), BF16),
            pltpu.VMEM((GROUP * TILE, 64), BF16),
            pltpu.VMEM((96, GROUP * TILE), BF16),
            pltpu.VMEM((96, GROUP * TILE), BF16),
            pltpu.VMEM((GROUP * TILE, segments), BF16),
            pltpu.VMEM((GROUP * TILE, segments), BF16),
            pltpu.VMEM((GROUP * TILE, segments), BF16),
            pltpu.VMEM((GROUP * TILE, segments), BF16),
            pltpu.SMEM((3 * extent + 8, 128), jnp.int32),
            pltpu.SMEM((blocks, most), jnp.int32),
            pltpu.SMEM((blocks,), jnp.int32),
            pltpu.SemaphoreType.DMA((2,)),
        ],
        compiler_params=pltpu.CompilerParams(vmem_limit_bytes=60 << 20),
        name="pair_sums",
    )(meta, window)
    return tuple(jnp.transpose(grad, (1, 0, 2))[None] for grad in grads)


def solution(mesh):
    placed = (
        P("slab", "cells", None, None),
        P("slab", "cells", None, None),
        P("slab", "cells", None),
        P("slab", "cells"),
        P("slab", "cells", None),
        P("slab", "cells"),
    )
    return jax.shard_map(
        per_device,
        mesh=mesh,
        in_specs=placed,
        out_specs=(P("slab", "cells", None, None), P("slab", "cells", None, None)),
        check_vma=False,
    )
```

```python
import functools
import math

import jax
import jax.numpy as jnp
from jax import lax
from jax.experimental import pallas as pl
from jax.experimental.pallas import tpu as pltpu
from jax.sharding import PartitionSpec as P

REACH = 2
WIDTH_SQUARE = 4.0
SCALE = math.sqrt(2.0 * math.log2(math.e) / WIDTH_SQUARE)
F32, BF16 = jnp.float32, jnp.bfloat16
MESH = pl.DeviceIdType.MESH
TILE = 128
GROUP = 4
STRIP = 256
SIDES = ((-1, 0), (1, 0), (0, -1), (0, 1))


def when(condition, action):
    pl.when(condition)(action)


def gather_kernel(blocks, slots, cen, tan, wts, cnt, prs, pcn, win, meta, send_sem, recv_sem):
    cells, slabs = lax.axis_size("cells"), lax.axis_size("slab")
    c, s = lax.axis_index("cells"), lax.axis_index("slab")
    segments = win.shape[2]
    extent = blocks + 2 * REACH
    own = extent + REACH
    there = {(-1, 0): s > 0, (1, 0): s < slabs - 1, (0, -1): c > 0, (0, 1): c < cells - 1}

    def device(ds, dc):
        return {
            "slab": lax.rem(s + ds + slabs, slabs),
            "cells": lax.rem(c + dc + cells, cells),
        }

    barrier = pltpu.get_barrier_semaphore()
    for side in SIDES:

        def greet(side=side):
            pl.semaphore_signal(
                barrier, inc=1, device_id=device(*side), device_id_type=MESH
            )

        when(there[side], greet)

    def clear(first, count):
        def store():
            win[pl.ds(first, count)] = jnp.zeros((count,) + win.shape[1:], F32)

        return store

    when(s == 0, clear(0, extent))
    when(s == slabs - 1, clear(2 * extent, extent))
    for level in range(3):
        when(c == 0, clear(level * extent, REACH))
        when(c == cells - 1, clear(level * extent + REACH + blocks, REACH))

    lane = lax.broadcasted_iota(jnp.int32, (1, segments), 1)
    table = jnp.zeros((1, segments), jnp.int32)
    for k in range(slots):
        table = jnp.where(lane == k, prs[0, k], table)
        table = jnp.where(lane == slots + k, prs[1, k], table)
    table = jnp.where(lane == 2 * slots, pcn[0, 0], table)
    for b in range(blocks):
        for k in range(3):
            win[own + b, k : k + 1, :] = cen[k, b : b + 1, :]
            win[own + b, 3 + k : 4 + k, :] = tan[k, b : b + 1, :]
        win[own + b, 6:7, :] = jnp.where(lane < cnt[0, b], wts[0, b : b + 1, :], 0.0)
        row = jnp.where(lane == 2 * slots + 1, cnt[0, b], table)
        win[own + b, 7:8, :] = row.astype(F32)
    pl.semaphore_wait(barrier, sum(there[side].astype(jnp.int32) for side in SIDES))

    used = iter(range(send_sem.shape[0]))

    def copy(source, target, count, side):
        n = next(used)
        return pltpu.make_async_remote_copy(
            src_ref=win.at[pl.ds(source, count)],
            dst_ref=win.at[pl.ds(target, count)],
            send_sem=send_sem.at[n],
            recv_sem=recv_sem.at[n],
            device_id=device(*side),
            device_id_type=MESH,
        )

    rims = {-1: 0, 1: blocks - REACH}
    halos = {-1: REACH + blocks, 1: 0}
    first_hop, second_hop = [], []
    for ds in (-1, 1):
        for dc in (-1, 1):
            block = rims[dc]
            one = copy(own + block, (1 - ds) * extent + REACH + block, REACH, (ds, 0))
            when(there[ds, 0], one.start)
            first_hop.append((ds, dc, one))
    beside = []
    for dc in (-1, 1):
        one = copy(own + rims[dc], extent + halos[dc], REACH, (0, dc))
        when(there[0, dc], one.start)
        beside.append((dc, one))
    for ds, dc, one in first_hop:
        came = there[-ds, 0]
        when(came, one.wait_recv)
        level = (1 - ds) * extent
        more = copy(level + REACH + rims[dc], level + halos[dc], REACH, (0, dc))
        when(came & there[0, dc], more.start)
        second_hop.append((came, dc, more))
    for ds, dc, one in first_hop:
        when(there[ds, 0], one.wait_send)
    for dc, one in beside:
        when(there[0, dc], one.wait_send)
        when(there[0, -dc], one.wait_recv)
    for came, dc, more in second_hop:
        when(came & there[0, dc], more.wait_send)
        when(came & there[0, -dc], more.wait_recv)
    for slot in range(3 * extent):
        meta[slot : slot + 1, :] = win[slot, 7:8, 0:128].astype(jnp.int32)
    meta[3 * extent : 3 * extent + 8, :] = jnp.full((8, 128), c, jnp.int32)


def pieces(value):
    high = value.astype(BF16).astype(F32)
    rest = value - high
    middle = rest.astype(BF16).astype(F32)
    return high, middle, rest - middle


def spread(tile, row):
    return jnp.broadcast_to(tile[row : row + 1], tile.shape)


def position_rows(tile, norm_row, one_row):
    row = lax.broadcasted_iota(jnp.int32, tile.shape, 0)
    x, y, z = [spread(tile, r) * SCALE for r in range(3)]
    norm = -0.5 * (x * x + y * y + z * z)
    base = jnp.where(row < 3, tile * SCALE, 0.0)
    return jnp.where(row == norm_row, norm, jnp.where(row == one_row, 1.0, base))


def tangent_products(tile):
    row = lax.broadcasted_iota(jnp.int32, tile.shape, 0)
    t0, t1, t2 = [spread(tile, r) for r in range(3, 6)]
    left = jnp.where(row < 3, t0, jnp.where(row < 5, t1, t2))
    right = jnp.where(row == 0, t0, jnp.where((row == 1) | (row == 3), t1, t2))
    return left * right, row


def prepare_own(win, slot, vr, p):
    p1, p2, p3 = pieces(position_rows(win[slot], 4, 3))
    vr[p] = jnp.concatenate([p1, p2, p1, p2, p3, p1, p3, p2], axis=0).astype(BF16)


def prepare_unit(win, places, ut, ft):
    tile = jnp.concatenate([win[slot, :, pl.ds(start, TILE)] for slot, start in places], axis=1)
    q1, q2, q3 = pieces(position_rows(tile, 3, 4))
    ut[...] = jnp.concatenate([q1, q1, q2, q2, q1, q3, q2, q3], axis=0).T.astype(BF16)
    products, row = tangent_products(tile)
    base = jnp.where(row < 6, spread(tile, 6) * products, 0.0)
    terms = jnp.concatenate([base] + [base * spread(tile, k) for k in range(3)], axis=0)
    ft[...] = jnp.concatenate(pieces(terms), axis=0).astype(BF16)


def dot(a, b):
    return lax.dot_general(a, b, (((1,), (0,)), ((), ())), preferred_element_type=F32)


def gauss_step(ut, vr, p, high, low, cols):
    gauss = jnp.exp2(dot(ut[...], vr[p, :, cols]))
    top = gauss.astype(BF16)
    high[:, cols] = top
    low[:, cols] = (gauss - top.astype(F32)).astype(BF16)


def sum_step(ft, high, low, acc, p, cols):
    whole = dot(ft[...], high[:, cols])
    part = dot(ft[0:32], low[:, cols])
    acc[p, :, cols] += whole[0:32] + whole[32:64] + whole[64:96] + part


def pair_kernel(
    blocks, slots, meta_hbm, win_hbm, gc, gt, win, acc, vr, ut0, ut1, f0, f1, h0, h1, l0, l1,
    meta, units, order, counts, ends, sems,
):
    table_copy = pltpu.make_async_copy(meta_hbm, meta, sems.at[0])
    window_copy = pltpu.make_async_copy(
        win_hbm, win.at[pl.ds(0, win_hbm.shape[0])], sems.at[1]
    )
    table_copy.start()
    window_copy.start()
    acc[...] = jnp.zeros_like(acc)
    win[win_hbm.shape[0]] = jnp.zeros(win.shape[1:], F32)
    table_copy.wait()
    segments = win.shape[2]
    extent = blocks + 2 * REACH
    own = extent + REACH
    chunks = segments // TILE
    cells = lax.axis_size("cells")
    slab_blocks = blocks * cells
    c = meta[3 * extent, 0]
    anchor = c * blocks - REACH
    low_own = c * blocks

    for p in range(blocks):
        counts[p] = 0

    def append(p, slot):
        at = counts[p]
        live = lax.div(meta[slot, 2 * slots + 1] + (TILE - 1), TILE)

        for k in range(chunks):
            units[p, at + k] = slot * chunks + k
        counts[p] = at + live

    def list_source(level, side):
        slot0 = (level + 1) * extent + {-1: 0, 0: REACH, 1: REACH + blocks}[side]

        def one(k, carry):
            first = meta[slot0, k]
            second = meta[slot0, slots + k]
            upper = second >= slab_blocks
            if level == 0 and side == 0:
                inside = jnp.where(upper, second - slab_blocks, second)
                append(
                    first - low_own, jnp.where(upper, 2 * extent, extent) + inside - anchor
                )
            target = second - slab_blocks if level < 0 else second
            wanted = (target >= low_own) & (target < low_own + blocks)
            if level == 0:
                wanted = wanted & jnp.logical_not(upper)
            if level == 0 and side == 0:
                wanted = wanted & (first != second)

            @pl.when(wanted)
            def _():
                append(target - low_own, (level + 1) * extent + first - anchor)

            return carry

        lax.fori_loop(0, meta[slot0, 2 * slots], one, 0)

    list_source(0, 0)
    for side in (-1, 1):
        has = c > 0 if side < 0 else c < cells - 1
        pl.when(has)(functools.partial(list_source, 0, side))
        pl.when(has)(functools.partial(list_source, -1, side))
    list_source(-1, 0)

    window_copy.wait()
    for p in range(blocks):
        prepare_own(win, own + p, vr, p)

    uts, fts, highs, lows = (ut0, ut1), (f0, f1), (h0, h1), (l0, l1)

    null = 3 * extent * chunks
    half_order = order.shape[0] // 2

    def list_units(p, at):
        for k in range(3 * GROUP):
            units[p, counts[p] + k] = null
        total = lax.div(counts[p] + GROUP - 1, GROUP)

        def one(u, carry):
            order[at + u] = p
            order[half_order + at + u] = GROUP * u
            return carry

        lax.fori_loop(0, total, one, 0)
        ends[p] = at + total
        return at + total

    total = lax.fori_loop(0, blocks, list_units, 0)
    for k in range(2):
        order[total + k] = blocks - 1
        order[half_order + total + k] = counts[blocks - 1] + GROUP * k

    def places(g):
        p, first = order[g], order[half_order + g]
        found = []
        for k in range(GROUP):
            unit = units[p, first + k]
            start = pl.multiple_of(lax.rem(unit, chunks) * TILE, TILE)
            found.append((lax.div(unit, chunks), start))
        return found

    def strips(width):
        return [slice(i, min(i + STRIP, width)) for i in range(0, width, STRIP)]

    prepare_unit(win, places(0), uts[0], fts[0])
    for cols in strips(segments):
        gauss_step(uts[0], vr, order[0], highs[0], lows[0], cols)
    prepare_unit(win, places(1), uts[1], fts[1])

    def run(width, p, start, stop):
        def half(k, g):
            n = 1 - k
            ahead = order[g + 1]
            for cols in strips(width):
                sum_step(fts[k], highs[k], lows[k], acc, p, cols)
                gauss_step(uts[n], vr, ahead, highs[n], lows[n], cols)
            prepare_unit(win, places(g + 2), uts[k], fts[k])

        def body(g, carry):
            parity = lax.rem(g, 2)
            pl.when(parity == 0)(functools.partial(half, 0, g))
            pl.when(parity == 1)(functools.partial(half, 1, g))
            return carry

        lax.fori_loop(start, stop, body, 0)

    def own_width(p):
        return lax.div(meta[own + p, 2 * slots + 1] + (TILE - 1), TILE)

    def one_block(p, start):
        stop = ends[p]
        width = own_width(p)
        for k in range(chunks // 2, chunks + 1):
            pl.when((width == k) & (stop > start))(
                functools.partial(run, k * TILE, p, start, stop)
            )
        following = order[stop]

        def widen(k, cols, carry):
            cols = pl.ds(pl.multiple_of(cols * TILE, TILE), TILE)
            gauss_step(uts[k], vr, following, highs[k], lows[k], cols)
            return carry

        for k in range(2):
            more = jnp.where(
                (lax.rem(stop, 2) == k) & (stop > start), own_width(following), 0
            )
            lax.fori_loop(width, more, functools.partial(widen, k), 0)
        return stop

    lax.fori_loop(0, blocks, one_block, 0)

    loss_scale = segments**-0.5
    for p in range(blocks):
        tile = win[own + p]
        products, row = tangent_products(tile)
        twice = jnp.where((row == 0) | (row == 3) | (row == 5), 1.0, 2.0)
        forms = jnp.where(row < 6, products * twice, 0.0)
        total = acc[p]
        weight = tile[6:7]
        sums = [
            jnp.sum(forms * total[8 * k : 8 * k + 8], axis=0, keepdims=True) for k in range(4)
        ]
        pull = (-4.0 * loss_scale / WIDTH_SQUARE) * weight
        for k in range(3):
            gc[k, p : p + 1, :] = pull * (tile[k : k + 1] * sums[0] - sums[k + 1])
        m = [total[k : k + 1] for k in range(6)]
        t = [tile[k : k + 1] for k in range(3, 6)]
        turn = (4.0 * loss_scale) * weight
        for k, (x, y, z) in enumerate(((0, 1, 2), (1, 3, 4), (2, 4, 5))):
            gt[k, p : p + 1, :] = turn * (m[x] * t[0] + m[y] * t[1] + m[z] * t[2])


def per_device(centres, tangents, weights, segment_count, pairs, pair_count):
    blocks, segments, slots = centres.shape[1], centres.shape[3], pairs.shape[1]
    extent = blocks + 2 * REACH
    vmem = pl.BlockSpec(memory_space=pltpu.VMEM)
    smem = pl.BlockSpec(memory_space=pltpu.SMEM)
    window, meta = pl.pallas_call(
        functools.partial(gather_kernel, blocks, slots),
        out_shape=(
            jax.ShapeDtypeStruct((3 * extent, 8, segments), F32),
            jax.ShapeDtypeStruct((3 * extent + 8, 128), jnp.int32),
        ),
        in_specs=[vmem, vmem, vmem, smem, smem, smem],
        out_specs=(vmem, vmem),
        scratch_shapes=[
            pltpu.SemaphoreType.DMA((10,)),
            pltpu.SemaphoreType.DMA((10,)),
        ],
        compiler_params=pltpu.CompilerParams(collective_id=0, has_side_effects=True),
        name="gather_window",
    )(
        jnp.transpose(centres[0], (1, 0, 2)),
        jnp.transpose(tangents[0], (1, 0, 2)),
        weights,
        segment_count,
        jnp.transpose(pairs[0]),
        pair_count,
    )
    most = (2 * REACH + 1) * 3 * (segments // TILE) + 3 * GROUP
    hbm = pl.BlockSpec(memory_space=pltpu.HBM)
    grads = pl.pallas_call(
        functools.partial(pair_kernel, blocks, slots),
        out_shape=(
            jax.ShapeDtypeStruct((3, blocks, segments), F32),
            jax.ShapeDtypeStruct((3, blocks, segments), F32),
        ),
        in_specs=[hbm, hbm],
        out_specs=(vmem, vmem),
        scratch_shapes=[
            pltpu.VMEM((3 * extent + 1, 8, segments), F32),
            pltpu.VMEM((blocks, 32, segments), F32),
            pltpu.VMEM((blocks, 64, segments), BF16),
            pltpu.VMEM((GROUP * TILE, 64), BF16),
            pltpu.VMEM((GROUP * TILE, 64), BF16),
            pltpu.VMEM((96, GROUP * TILE), BF16),
            pltpu.VMEM((96, GROUP * TILE), BF16),
            pltpu.VMEM((GROUP * TILE, segments), BF16),
            pltpu.VMEM((GROUP * TILE, segments), BF16),
            pltpu.VMEM((GROUP * TILE, segments), BF16),
            pltpu.VMEM((GROUP * TILE, segments), BF16),
            pltpu.SMEM((3 * extent + 8, 128), jnp.int32),
            pltpu.SMEM((blocks, most), jnp.int32),
            pltpu.SMEM((2 * blocks * most,), jnp.int32),
            pltpu.SMEM((blocks,), jnp.int32),
            pltpu.SMEM((blocks,), jnp.int32),
            pltpu.SemaphoreType.DMA((2,)),
        ],
        compiler_params=pltpu.CompilerParams(vmem_limit_bytes=60 << 20),
        name="pair_sums",
    )(meta, window)
    return tuple(jnp.transpose(grad, (1, 0, 2))[None] for grad in grads)


def solution(mesh):
    placed = (
        P("slab", "cells", None, None),
        P("slab", "cells", None, None),
        P("slab", "cells", None),
        P("slab", "cells"),
        P("slab", "cells", None),
        P("slab", "cells"),
    )
    return jax.shard_map(
        per_device,
        mesh=mesh,
        in_specs=placed,
        out_specs=(P("slab", "cells", None, None), P("slab", "cells", None, None)),
        check_vma=False,
    )
```

```python
import functools
import math

import jax
import jax.numpy as jnp
from jax import lax
from jax.experimental import pallas as pl
from jax.experimental.pallas import tpu as pltpu
from jax.sharding import PartitionSpec as P

REACH = 2
WIDTH_SQUARE = 4.0
SCALE = math.sqrt(2.0 * math.log2(math.e) / WIDTH_SQUARE)
F32, BF16 = jnp.float32, jnp.bfloat16
MESH = pl.DeviceIdType.MESH
TILE = 128
GROUP = 4
STRIP = 256
SIDES = ((-1, 0), (1, 0), (0, -1), (0, 1))


def when(condition, action):
    pl.when(condition)(action)


def gather_kernel(blocks, slots, cen, tan, wts, cnt, prs, pcn, win, meta, send_sem, recv_sem):
    cells, slabs = lax.axis_size("cells"), lax.axis_size("slab")
    c, s = lax.axis_index("cells"), lax.axis_index("slab")
    segments = win.shape[2]
    extent = blocks + 2 * REACH
    own = extent + REACH
    there = {(-1, 0): s > 0, (1, 0): s < slabs - 1, (0, -1): c > 0, (0, 1): c < cells - 1}

    def device(ds, dc):
        return {
            "slab": lax.rem(s + ds + slabs, slabs),
            "cells": lax.rem(c + dc + cells, cells),
        }

    barrier = pltpu.get_barrier_semaphore()
    for side in SIDES:

        def greet(side=side):
            pl.semaphore_signal(
                barrier, inc=1, device_id=device(*side), device_id_type=MESH
            )

        when(there[side], greet)

    def clear(first, count):
        def store():
            win[pl.ds(first, count)] = jnp.zeros((count,) + win.shape[1:], F32)

        return store

    when(s == 0, clear(0, extent))
    when(s == slabs - 1, clear(2 * extent, extent))
    for level in range(3):
        when(c == 0, clear(level * extent, REACH))
        when(c == cells - 1, clear(level * extent + REACH + blocks, REACH))

    lane = lax.broadcasted_iota(jnp.int32, (1, segments), 1)
    table = jnp.zeros((1, segments), jnp.int32)
    for k in range(slots):
        table = jnp.where(lane == k, prs[0, k], table)
        table = jnp.where(lane == slots + k, prs[1, k], table)
    table = jnp.where(lane == 2 * slots, pcn[0, 0], table)
    for b in range(blocks):
        for k in range(3):
            win[own + b, k : k + 1, :] = cen[k, b : b + 1, :]
            win[own + b, 3 + k : 4 + k, :] = tan[k, b : b + 1, :]
        win[own + b, 6:7, :] = jnp.where(lane < cnt[0, b], wts[0, b : b + 1, :], 0.0)
        row = jnp.where(lane == 2 * slots + 1, cnt[0, b], table)
        win[own + b, 7:8, :] = row.astype(F32)
    pl.semaphore_wait(barrier, sum(there[side].astype(jnp.int32) for side in SIDES))

    used = iter(range(send_sem.shape[0]))

    def copy(source, target, count, side):
        n = next(used)
        return pltpu.make_async_remote_copy(
            src_ref=win.at[pl.ds(source, count)],
            dst_ref=win.at[pl.ds(target, count)],
            send_sem=send_sem.at[n],
            recv_sem=recv_sem.at[n],
            device_id=device(*side),
            device_id_type=MESH,
        )

    rims = {-1: 0, 1: blocks - REACH}
    halos = {-1: REACH + blocks, 1: 0}
    first_hop, second_hop = [], []
    for ds in (-1, 1):
        for dc in (-1, 1):
            block = rims[dc]
            one = copy(own + block, (1 - ds) * extent + REACH + block, REACH, (ds, 0))
            when(there[ds, 0], one.start)
            first_hop.append((ds, dc, one))
    beside = []
    for dc in (-1, 1):
        one = copy(own + rims[dc], extent + halos[dc], REACH, (0, dc))
        when(there[0, dc], one.start)
        beside.append((dc, one))
    for ds, dc, one in first_hop:
        came = there[-ds, 0]
        when(came, one.wait_recv)
        level = (1 - ds) * extent
        more = copy(level + REACH + rims[dc], level + halos[dc], REACH, (0, dc))
        when(came & there[0, dc], more.start)
        second_hop.append((came, dc, more))
    for ds, dc, one in first_hop:
        when(there[ds, 0], one.wait_send)
    for dc, one in beside:
        when(there[0, dc], one.wait_send)
        when(there[0, -dc], one.wait_recv)
    for came, dc, more in second_hop:
        when(came & there[0, dc], more.wait_send)
        when(came & there[0, -dc], more.wait_recv)
    for slot in range(3 * extent):
        meta[slot : slot + 1, :] = win[slot, 7:8, 0:128].astype(jnp.int32)
    meta[3 * extent : 3 * extent + 8, :] = jnp.full((8, 128), c, jnp.int32)


def pieces(value):
    high = value.astype(BF16).astype(F32)
    rest = value - high
    middle = rest.astype(BF16).astype(F32)
    return high, middle, rest - middle


def spread(tile, row):
    return jnp.broadcast_to(tile[row : row + 1], tile.shape)


def position_rows(tile, norm_row, one_row):
    row = lax.broadcasted_iota(jnp.int32, tile.shape, 0)
    x, y, z = [spread(tile, r) * SCALE for r in range(3)]
    norm = -0.5 * (x * x + y * y + z * z)
    base = jnp.where(row < 3, tile * SCALE, 0.0)
    return jnp.where(row == norm_row, norm, jnp.where(row == one_row, 1.0, base))


def tangent_products(tile):
    row = lax.broadcasted_iota(jnp.int32, tile.shape, 0)
    t0, t1, t2 = [spread(tile, r) for r in range(3, 6)]
    left = jnp.where(row < 3, t0, jnp.where(row < 5, t1, t2))
    right = jnp.where(row == 0, t0, jnp.where((row == 1) | (row == 3), t1, t2))
    return left * right, row


def prepare_own(win, slot, vr, p):
    p1, p2, p3 = pieces(position_rows(win[slot], 4, 3))
    vr[p] = jnp.concatenate([p1, p2, p1, p2, p3, p1, p3, p2], axis=0).astype(BF16)


def prepare_unit(win, places, ut, ft):
    tile = jnp.concatenate([win[slot, :, pl.ds(start, TILE)] for slot, start in places], axis=1)
    q1, q2, q3 = pieces(position_rows(tile, 3, 4))
    ut[...] = jnp.concatenate([q1, q1, q2, q2, q1, q3, q2, q3], axis=0).T.astype(BF16)
    products, row = tangent_products(tile)
    base = jnp.where(row < 6, spread(tile, 6) * products, 0.0)
    terms = jnp.concatenate([base] + [base * spread(tile, k) for k in range(3)], axis=0)
    ft[...] = jnp.concatenate(pieces(terms), axis=0).astype(BF16)


def dot(a, b):
    return lax.dot_general(a, b, (((1,), (0,)), ((), ())), preferred_element_type=F32)


def gauss_step(ut, vr, p, high, low, cols):
    gauss = jnp.exp2(dot(ut[...], vr[p, :, cols]))
    top = gauss.astype(BF16)
    high[:, cols] = top
    low[:, cols] = (gauss - top.astype(F32)).astype(BF16)


def sum_step(ft, high, low, acc, p, cols):
    whole = dot(ft[...], high[:, cols])
    part = dot(ft[0:32], low[:, cols])
    acc[p, :, cols] += whole[0:32] + whole[32:64] + whole[64:96] + part


def pair_kernel(
    blocks, slots, meta_hbm, win_hbm, gc, gt, win, acc, vr, ut0, ut1, f0, f1, h0, h1, l0, l1,
    meta, units, order, counts, ends, sems,
):
    table_copy = pltpu.make_async_copy(meta_hbm, meta, sems.at[0])
    window_copy = pltpu.make_async_copy(
        win_hbm, win.at[pl.ds(0, win_hbm.shape[0])], sems.at[1]
    )
    table_copy.start()
    window_copy.start()
    acc[...] = jnp.zeros_like(acc)
    win[win_hbm.shape[0]] = jnp.zeros(win.shape[1:], F32)
    table_copy.wait()
    segments = win.shape[2]
    extent = blocks + 2 * REACH
    own = extent + REACH
    chunks = segments // TILE
    cells = lax.axis_size("cells")
    slab_blocks = blocks * cells
    c = meta[3 * extent, 0]
    anchor = c * blocks - REACH
    low_own = c * blocks

    for p in range(blocks):
        counts[p] = 0

    def append(p, slot):
        at = counts[p]
        live = lax.div(meta[slot, 2 * slots + 1] + (TILE - 1), TILE)

        for k in range(chunks):
            units[p, at + k] = slot * chunks + k
        counts[p] = at + live

    def list_source(level, side):
        slot0 = (level + 1) * extent + {-1: 0, 0: REACH, 1: REACH + blocks}[side]

        def one(k, carry):
            first = meta[slot0, k]
            second = meta[slot0, slots + k]
            upper = second >= slab_blocks
            if level == 0 and side == 0:
                inside = jnp.where(upper, second - slab_blocks, second)
                append(
                    first - low_own, jnp.where(upper, 2 * extent, extent) + inside - anchor
                )
            target = second - slab_blocks if level < 0 else second
            wanted = (target >= low_own) & (target < low_own + blocks)
            if level == 0:
                wanted = wanted & jnp.logical_not(upper)
            if level == 0 and side == 0:
                wanted = wanted & (first != second)

            @pl.when(wanted)
            def _():
                append(target - low_own, (level + 1) * extent + first - anchor)

            return carry

        lax.fori_loop(0, meta[slot0, 2 * slots], one, 0)

    list_source(0, 0)
    for side in (-1, 1):
        has = c > 0 if side < 0 else c < cells - 1
        pl.when(has)(functools.partial(list_source, 0, side))
        pl.when(has)(functools.partial(list_source, -1, side))
    list_source(-1, 0)

    window_copy.wait()
    for p in range(blocks):
        prepare_own(win, own + p, vr, p)

    uts, fts, highs, lows = (ut0, ut1), (f0, f1), (h0, h1), (l0, l1)

    null = 3 * extent * chunks
    half_order = order.shape[0] // 2

    def list_units(p, at):
        for k in range(3 * GROUP):
            units[p, counts[p] + k] = null
        total = lax.div(counts[p] + GROUP - 1, GROUP)

        def one(u, carry):
            order[at + u] = p
            order[half_order + at + u] = GROUP * u
            return carry

        lax.fori_loop(0, total, one, 0)
        ends[p] = at + total
        return at + total

    total = lax.fori_loop(0, blocks, list_units, 0)
    for k in range(2):
        order[total + k] = blocks - 1
        order[half_order + total + k] = counts[blocks - 1] + GROUP * k

    def places(g):
        p, first = order[g], order[half_order + g]
        found = []
        for k in range(GROUP):
            unit = units[p, first + k]
            start = pl.multiple_of(lax.rem(unit, chunks) * TILE, TILE)
            found.append((lax.div(unit, chunks), start))
        return found

    def strips(width):
        return [slice(i, min(i + STRIP, width)) for i in range(0, width, STRIP)]

    prepare_unit(win, places(0), uts[0], fts[0])
    for cols in strips(segments):
        gauss_step(uts[0], vr, order[0], highs[0], lows[0], cols)
    prepare_unit(win, places(1), uts[1], fts[1])

    def run(width, p, start, stop):
        def half(k, g):
            n = 1 - k
            ahead = order[g + 1]
            for cols in strips(width):
                sum_step(fts[k], highs[k], lows[k], acc, p, cols)
                gauss_step(uts[n], vr, ahead, highs[n], lows[n], cols)
            prepare_unit(win, places(g + 2), uts[k], fts[k])

        def body(g, carry):
            parity = lax.rem(g, 2)
            pl.when(parity == 0)(functools.partial(half, 0, g))
            pl.when(parity == 1)(functools.partial(half, 1, g))
            return carry

        lax.fori_loop(start, stop, body, 0)

    def own_width(p):
        width = lax.div(meta[own + p, 2 * slots + 1] + (TILE - 1), TILE)
        return jnp.where(width == chunks - 1, chunks, width)

    def one_block(p, start):
        stop = ends[p]
        width = own_width(p)
        for k in range(chunks // 2, chunks + 1):
            if k == chunks - 1:
                continue
            pl.when((width == k) & (stop > start))(
                functools.partial(run, k * TILE, p, start, stop)
            )
        following = order[stop]

        def widen(k, cols, carry):
            cols = pl.ds(pl.multiple_of(cols * TILE, TILE), TILE)
            gauss_step(uts[k], vr, following, highs[k], lows[k], cols)
            return carry

        for k in range(2):
            more = jnp.where(
                (lax.rem(stop, 2) == k) & (stop > start), own_width(following), 0
            )
            lax.fori_loop(width, more, functools.partial(widen, k), 0)
        return stop

    lax.fori_loop(0, blocks, one_block, 0)

    loss_scale = segments**-0.5
    for p in range(blocks):
        tile = win[own + p]
        products, row = tangent_products(tile)
        twice = jnp.where((row == 0) | (row == 3) | (row == 5), 1.0, 2.0)
        forms = jnp.where(row < 6, products * twice, 0.0)
        total = acc[p]
        weight = tile[6:7]
        sums = [
            jnp.sum(forms * total[8 * k : 8 * k + 8], axis=0, keepdims=True) for k in range(4)
        ]
        pull = (-4.0 * loss_scale / WIDTH_SQUARE) * weight
        for k in range(3):
            gc[k, p : p + 1, :] = pull * (tile[k : k + 1] * sums[0] - sums[k + 1])
        m = [total[k : k + 1] for k in range(6)]
        t = [tile[k : k + 1] for k in range(3, 6)]
        turn = (4.0 * loss_scale) * weight
        for k, (x, y, z) in enumerate(((0, 1, 2), (1, 3, 4), (2, 4, 5))):
            gt[k, p : p + 1, :] = turn * (m[x] * t[0] + m[y] * t[1] + m[z] * t[2])


def per_device(centres, tangents, weights, segment_count, pairs, pair_count):
    blocks, segments, slots = centres.shape[1], centres.shape[3], pairs.shape[1]
    extent = blocks + 2 * REACH
    vmem = pl.BlockSpec(memory_space=pltpu.VMEM)
    smem = pl.BlockSpec(memory_space=pltpu.SMEM)
    window, meta = pl.pallas_call(
        functools.partial(gather_kernel, blocks, slots),
        out_shape=(
            jax.ShapeDtypeStruct((3 * extent, 8, segments), F32),
            jax.ShapeDtypeStruct((3 * extent + 8, 128), jnp.int32),
        ),
        in_specs=[vmem, vmem, vmem, smem, smem, smem],
        out_specs=(vmem, vmem),
        scratch_shapes=[
            pltpu.SemaphoreType.DMA((10,)),
            pltpu.SemaphoreType.DMA((10,)),
        ],
        compiler_params=pltpu.CompilerParams(collective_id=0, has_side_effects=True),
        name="gather_window",
    )(
        jnp.transpose(centres[0], (1, 0, 2)),
        jnp.transpose(tangents[0], (1, 0, 2)),
        weights,
        segment_count,
        jnp.transpose(pairs[0]),
        pair_count,
    )
    most = (2 * REACH + 1) * 3 * (segments // TILE) + 3 * GROUP
    hbm = pl.BlockSpec(memory_space=pltpu.HBM)
    grads = pl.pallas_call(
        functools.partial(pair_kernel, blocks, slots),
        out_shape=(
            jax.ShapeDtypeStruct((3, blocks, segments), F32),
            jax.ShapeDtypeStruct((3, blocks, segments), F32),
        ),
        in_specs=[hbm, hbm],
        out_specs=(vmem, vmem),
        scratch_shapes=[
            pltpu.VMEM((3 * extent + 1, 8, segments), F32),
            pltpu.VMEM((blocks, 32, segments), F32),
            pltpu.VMEM((blocks, 64, segments), BF16),
            pltpu.VMEM((GROUP * TILE, 64), BF16),
            pltpu.VMEM((GROUP * TILE, 64), BF16),
            pltpu.VMEM((96, GROUP * TILE), BF16),
            pltpu.VMEM((96, GROUP * TILE), BF16),
            pltpu.VMEM((GROUP * TILE, segments), BF16),
            pltpu.VMEM((GROUP * TILE, segments), BF16),
            pltpu.VMEM((GROUP * TILE, segments), BF16),
            pltpu.VMEM((GROUP * TILE, segments), BF16),
            pltpu.SMEM((3 * extent + 8, 128), jnp.int32),
            pltpu.SMEM((blocks, most), jnp.int32),
            pltpu.SMEM((2 * blocks * most,), jnp.int32),
            pltpu.SMEM((blocks,), jnp.int32),
            pltpu.SMEM((blocks,), jnp.int32),
            pltpu.SemaphoreType.DMA((2,)),
        ],
        compiler_params=pltpu.CompilerParams(vmem_limit_bytes=60 << 20),
        name="pair_sums",
    )(meta, window)
    return tuple(jnp.transpose(grad, (1, 0, 2))[None] for grad in grads)


def solution(mesh):
    placed = (
        P("slab", "cells", None, None),
        P("slab", "cells", None, None),
        P("slab", "cells", None),
        P("slab", "cells"),
        P("slab", "cells", None),
        P("slab", "cells"),
    )
    return jax.shard_map(
        per_device,
        mesh=mesh,
        in_specs=placed,
        out_specs=(P("slab", "cells", None, None), P("slab", "cells", None, None)),
        check_vma=False,
    )
```
